32 devices in a mesh: ens: 2 (over x), lat: 16 (over z, y, core).
Axes of the slice: x: 2, y: 2, z: 4, core: 2. Of those that a mesh axis runs over, the one named last changes fastest.
Arguments:
- atmos: bfloat16 [11520, 1024], P(('ens', 'lat')), parts along dimension 0, may hold values from -6 to 6
- ocean_state: bfloat16 [76, 128, 1440], P(None, ('ens', 'lat')), parts along dimension 1, may hold values from -6 to 6
- land_mask: int32 [64, 1440], P('lat'), may hold values 0 or 1
- w_qkv: bfloat16 [1024, 3072], replicated, may hold values from -0.1875 to 0.1875
- w_out: bfloat16 [1024, 1024], replicated, may hold values from -0.1875 to 0.1875
- head_scale: float32 [16], replicated, may hold values from 0.5 to 80
- gain_attn: float32 [1024], replicated, may hold values from 0.5 to 1.5
- gain_flux: float32 [1024], replicated, may hold values from 0.1 to 1.9
- w_flux: bfloat16 [1024, 16], replicated, may hold values from -0.1875 to 0.1875
- surf_embed: float32 [4, 1024], replicated, may hold values from -3 to 3
- flux_start: int32 [64], P('lat'), may hold values from 0 to 14, as said below
- flux_weight: float32 [64, 2], P('lat'), may hold values from 0.25 to 1
- surf_start: int32 [16], P('lat'), may hold values from -2 to 59, as said below
- surf_weight: float32 [16, 7], P('lat'), may hold values from 0.1 to 0.5
- conv_first: bfloat16 [9, 128, 92], replicated, may hold values from -0.21875 to 0.21875
- conv_second: bfloat16 [9, 76, 128], replicated, may hold values from -0.1875 to 0.1875
Outputs:
- atmos_next: bfloat16 [11520, 1024], P(('ens', 'lat')), parts along dimension 0
- ocean_next: bfloat16 [76, 128, 1440], P(None, ('ens', 'lat')), parts along dimension 1
The draws below stay inside these ranges and needn't reach their ends.
There are 2 independent parts, one for each index of `ens`. The reference program is written for one: setup_inputs(seed, part) draws one part's arguments, and reference() takes and returns one part's arrays. A program takes and returns all parts, laid end to end along the dimension named above; an argument that names none is the same for every part. Nothing has to cross between parts.
Inputs may be any that keep to these rules, and one draw needn't show every extreme that they name: flux_start[i] is i // 4 - 1 or i // 4, kept within 0 to 14. surf_start[r] is 4 r - 2 or 4 r - 1.
All inputs are finite; a program needn't handle non-finite values. No bound on the sum of `land_mask` on one device may be relied on, other than what follows from the above.
Results may differ from the reference program's by a relative error of at most 0.0065.
The reference program's roundings to bfloat16 on the way count: a program that leaves them out, or rounds other values in their place, can miss the bound.
Values may be sent and summed in bfloat16 or wider, within the bound.
A program may use at most 128 MiB of HBM per device.

```python
import jax
import jax.numpy as jnp
from jax import lax

D = 1024
HEADS = 16
NFLUX = 16
LEVELS = 19
VARS = 4
OCH = 76
HID = 128
ALON = 360
SPAN = 4
OLON = 1440
RATIO = 4
AROWS = 16
OROWS = 64
TOKENS = 5760
FBAND = 2
OBAND = 7
OSTEPS = 2


def draw_head_scale(key, part):
    lowest = jnp.log(jnp.float32(0.5))
    highest = jnp.log(jnp.float32(2.5))
    moderate = jnp.exp(jax.random.uniform(key, (HEADS,), jnp.float32, lowest, highest))
    return moderate


def draw_flux_start(key, part):
    ocean_rows = jnp.arange(OROWS, dtype=jnp.int32)
    jitter = jax.random.randint(key, (OROWS,), 0, 2, dtype=jnp.int32)
    return jnp.clip(ocean_rows // RATIO - 1 + jitter, 0, AROWS - FBAND).astype(jnp.int32)


def draw_surf_start(key, part):
    centres = jnp.arange(AROWS, dtype=jnp.int32) * RATIO
    jitter = jax.random.randint(key, (AROWS,), 0, 2, dtype=jnp.int32)
    return (centres - 2 + jitter).astype(jnp.int32)


def touch_ends(entries, rng, least, top_value):
    place = [jax.random.randint(jax.random.fold_in(rng, axis), (), 0, length) for axis, length in enumerate(entries.shape)]
    widest = entries.shape.index(max(entries.shape))
    beside = place[:widest] + [(place[widest] + 1) % entries.shape[widest]] + place[widest + 1:]
    return entries.at[tuple(place)].set(least).at[tuple(beside)].set(top_value)


def block_scale(rng, shape, cuts, smallest, top_value):
    loudness = 1.0
    for axis_at, shards_of in cuts:
        draws = jax.random.uniform(jax.random.fold_in(jax.random.fold_in(rng, 6), axis_at), (shards_of,), jnp.float32, smallest / len(cuts), top_value / len(cuts))
        loudness = loudness * jnp.repeat(jnp.exp(draws), shape[axis_at] // shards_of).reshape((-1,) + (1,) * (len(shape) - 1 - axis_at))
    return loudness


def bell_draw(stream_key, dims, scale, most, shards=(), held_as=jnp.bfloat16):
    loudness = block_scale(stream_key, dims, shards, -0.22, 0.18) if shards else 1.0
    entries = jax.random.normal(stream_key, dims, jnp.float32) * scale * loudness
    return jnp.minimum(jnp.maximum(entries, -most), most).astype(held_as)


def setup_inputs(seed: int = 0, part: int = 0) -> dict:
    seeds = jax.random.split(jax.random.key(seed), 17)
    part_splits = jax.random.split(jax.random.fold_in(seeds[16], part), 17)
    return {
        "atmos": bell_draw(part_splits[0], (TOKENS, D), 1.0, 6.0, ((0, 16),)),
        "ocean_state": bell_draw(part_splits[1], (OCH, OROWS, OLON), 1.0, 6.0, ((1, 16),)),
        "land_mask": touch_ends((jax.random.randint(seeds[2], (OROWS, OLON), 0, 10) < 7).astype(jnp.int32), jax.random.fold_in(seeds[2], 1), 0, 1),
        "w_qkv": bell_draw(seeds[3], (D, 3 * D), D ** -0.5, 0.1875),
        "w_out": bell_draw(seeds[4], (D, D), D ** -0.5, 0.1875),
        "head_scale": draw_head_scale(jax.random.fold_in(seeds[16], 71), part),
        "gain_attn": jnp.clip(1.0 + 0.1 * jax.random.normal(seeds[6], (D,), jnp.float32), 0.5, 1.5),
        "gain_flux": jnp.clip(1.0 + 0.18 * jax.random.normal(seeds[7], (D,), jnp.float32), 0.1, 1.9),
        "w_flux": bell_draw(seeds[8], (D, NFLUX), D ** -0.5, 0.1875),
        "surf_embed": bell_draw(seeds[9], (VARS, D), VARS ** -0.5, 3.0, (), jnp.float32),
        "flux_start": draw_flux_start(jax.random.fold_in(seeds[16], 71), part),
        "flux_weight": jnp.clip(0.25 + 0.75 * jax.random.uniform(seeds[11], (OROWS, FBAND), jnp.float32) ** block_scale(seeds[11], (OROWS, FBAND), ((0, 16),), -0.2, 0.2), 0.25, 1.0),
        "surf_start": draw_surf_start(jax.random.fold_in(seeds[16], 71), part),
        "surf_weight": jnp.clip(0.1 + 0.4 * jax.random.uniform(seeds[13], (AROWS, OBAND), jnp.float32) ** block_scale(seeds[13], (AROWS, OBAND), ((0, 16),), -0.2, 0.2), 0.1, 0.5),
        "conv_first": bell_draw(seeds[14], (9, HID, OCH + NFLUX), (9 * (OCH + NFLUX)) ** -0.5, 0.21875),
        "conv_second": bell_draw(seeds[15], (9, OCH, HID), (9 * HID) ** -0.5, 0.1875),
    }


def rms_norm(values, scaling):
    return values * lax.rsqrt(lax.optimization_barrier(jnp.mean(values * values, axis=-1, keepdims=True)) + 1e-06) * scaling

def band_matrix(starts, weight, first_col, col_count):
    columns = first_col + jnp.arange(col_count, dtype=jnp.int32)
    summed = jnp.zeros((starts.shape[0], col_count), jnp.float32)
    for offset in range(weight.shape[1]):
        matches = (columns[None, :] == starts[:, None] + offset).astype(jnp.float32)
        summed = summed + weight[:, offset:offset + 1] * matches
    return summed

def surface_rows(ocean_now):
    fields = ocean_now[0::LEVELS]
    averaged = lax.optimization_barrier(jnp.mean(fields.reshape(fields.shape[0], fields.shape[1], fields.shape[2] // SPAN, SPAN), axis=3))
    return averaged.transpose(1, 0, 2).reshape(fields.shape[1], -1)

def head_parts(qkv, head_scale):
    token_count = qkv.shape[0]
    width = qkv.shape[1] // 3
    head_count = head_scale.shape[0]
    depth = width // head_count
    query_raw = qkv[:, :width].reshape(token_count, head_count, depth)
    key_raw = qkv[:, width:2 * width].reshape(token_count, head_count, depth)
    query_part = query_raw * lax.rsqrt(lax.optimization_barrier(jnp.mean(query_raw * query_raw, axis=-1, keepdims=True)) + 1e-06)
    query_part = query_part * (head_scale[None, :, None] / jnp.sqrt(jnp.float32(depth)))
    key_part = key_raw * lax.rsqrt(lax.optimization_barrier(jnp.mean(key_raw * key_raw, axis=-1, keepdims=True)) + 1e-06)
    value_part = qkv[:, 2 * width:]
    return (query_part.astype(jnp.bfloat16), key_part.astype(jnp.bfloat16), value_part.astype(jnp.bfloat16))

def attend(query_rows, key_rows, value_rows, valid):
    key_count = key_rows.shape[0]
    scores = jnp.einsum('qhd,khd->hqk', query_rows.astype(jnp.float32), key_rows.astype(jnp.float32))
    scores = jnp.where(valid[None, None, :], scores, -1e+30)
    largest = lax.optimization_barrier(jnp.max(scores, axis=2, keepdims=True))
    raised = jnp.exp(scores - largest)
    probs = (raised / lax.optimization_barrier(jnp.sum(raised, axis=2, keepdims=True))).astype(jnp.bfloat16)
    value_heads = value_rows.reshape(key_count, key_rows.shape[1], key_rows.shape[2])
    mixed = jnp.einsum('hqk,khd->qhd', probs.astype(jnp.float32), value_heads.astype(jnp.float32))
    return mixed.astype(jnp.bfloat16).reshape(query_rows.shape[0], -1)

def spread_flux(regridded, flux_count):
    row_count = regridded.shape[0]
    shaped = regridded.reshape(row_count, -1, flux_count).transpose(2, 0, 1)
    return jnp.repeat(shaped, SPAN, axis=2).astype(jnp.bfloat16)

def convolve(padded, weight, row_count):
    channels = padded.shape[0]
    lon_count = padded.shape[2]
    summed = jnp.zeros((weight.shape[1], row_count * lon_count), jnp.float32)
    for tap_index in range(9):
        row_step = tap_index // 3 - 1
        lon_step = tap_index % 3 - 1
        shifted = jnp.roll(padded[:, 1 + row_step:1 + row_step + row_count, :], -lon_step, axis=2)
        summed = summed + jnp.dot(weight[tap_index], shifted.reshape(channels, -1), preferred_element_type=jnp.float32)
    return summed.reshape(weight.shape[1], row_count, lon_count)

def pad_rows(fields):
    return jnp.pad(fields, ((0, 0), (1, 1), (0, 0)))

def reference(atmos, ocean_state, land_mask, w_qkv, w_out, head_scale, gain_attn, gain_flux, w_flux, surf_embed, flux_start, flux_weight, surf_start, surf_weight, conv_first, conv_second):
    ocean_now = ocean_state.astype(jnp.float32)
    surface = surface_rows(ocean_now).astype(jnp.bfloat16)
    surf_matrix = band_matrix(surf_start, surf_weight, 0, OROWS)
    surf_atm = jnp.dot(surf_matrix, surface.astype(jnp.float32), precision=lax.Precision.HIGHEST)
    surf_tokens = surf_atm.reshape(AROWS, VARS, ALON).transpose(0, 2, 1).reshape(AROWS * ALON, VARS)
    start = atmos.astype(jnp.float32) + jnp.dot(surf_tokens, surf_embed, precision=lax.Precision.HIGHEST)
    normed = rms_norm(start, gain_attn).astype(jnp.bfloat16)
    qkv = jnp.dot(normed, w_qkv, preferred_element_type=jnp.float32)
    query_part, key_part, value_part = head_parts(qkv, head_scale)
    head_count = query_part.shape[1]
    depth = query_part.shape[2]
    query_grid = query_part.reshape(AROWS, ALON, head_count, depth)
    key_grid = jnp.pad(key_part.reshape(AROWS, ALON, head_count, depth), ((1, 1), (0, 0), (0, 0), (0, 0)))
    value_grid = jnp.pad(value_part.reshape(AROWS, ALON, D), ((1, 1), (0, 0), (0, 0)))

    def one_row(row_id):
        query_rows = lax.dynamic_slice_in_dim(query_grid, row_id, 1, 0)[0]
        key_rows = lax.dynamic_slice_in_dim(key_grid, row_id, 3, 0).reshape(3 * ALON, head_count, depth)
        value_rows = lax.dynamic_slice_in_dim(value_grid, row_id, 3, 0).reshape(3 * ALON, D)
        global_rows = row_id - 1 + jnp.arange(3 * ALON, dtype=jnp.int32) // ALON
        valid = (global_rows >= 0) & (global_rows < AROWS)
        return attend(query_rows, key_rows, value_rows, valid)
    mixed = lax.map(one_row, jnp.arange(AROWS, dtype=jnp.int32)).reshape(AROWS * ALON, D)
    after = start + jnp.dot(mixed, w_out, preferred_element_type=jnp.float32)
    atmos_next = after.astype(jnp.bfloat16)
    flux_in = rms_norm(after, gain_flux).astype(jnp.bfloat16)
    fluxes = jnp.dot(flux_in, w_flux, preferred_element_type=jnp.float32).astype(jnp.bfloat16).reshape(AROWS, ALON * NFLUX)
    flux_matrix = band_matrix(flux_start, flux_weight, 0, AROWS)
    regridded = jnp.dot(flux_matrix, fluxes.astype(jnp.float32), precision=lax.Precision.HIGHEST)
    ocean_flux = spread_flux(regridded, NFLUX)
    sea_cells = land_mask.astype(jnp.float32)
    for step_index in range(OSTEPS):
        inputs = jnp.concatenate([ocean_now.astype(jnp.bfloat16), ocean_flux], axis=0)
        hidden = jax.nn.gelu(convolve(pad_rows(inputs), conv_first, OROWS), approximate=True).astype(jnp.bfloat16)
        ocean_now = ocean_now + sea_cells[None] * convolve(pad_rows(hidden), conv_second, OROWS)
    return (atmos_next, ocean_now.astype(jnp.bfloat16))
```

```python
import jax
import jax.numpy as jnp
from jax import lax
from jax.experimental import pallas as pl
from jax.experimental.pallas import tpu as pltpu
from jax.sharding import PartitionSpec as P

LEVELS = 19
VARS = 4
SPAN = 4
OSTEPS = 2
GROUP = 256
CHUNK = 512
FAST, OWN, SLOW = 0, 1, 2


def round_up(value, unit):
    return (value + unit - 1) // unit * unit


def rms_norm(values, scaling):
    return values * lax.rsqrt(jnp.mean(values * values, axis=-1, keepdims=True) + 1e-06) * scaling


def step_kernel(surf_first, surf_weight, flux_first, flux_weight, scale_ref, land_ref, embed_ref,
                gain_ref, flux_gain_ref, wflux_ref, atmos_hbm, ocean_hbm, qkv_hbm, wout_hbm,
                first_hbm, second_hbm,
                after_ref, out_ref,
                ocean_in, atmos_in, first_in, second_in, surf, near, queries, keys, vals, keys_wide,
                vals_wide, probs, largest_at, total_at, rows, mid, land, sea,
                line, xs, fx, hs, st, kept, turned, w_state, w_flux, w_second,
                load_sems, send_sems, recv_sems, kv_send, kv_recv, halo_send, halo_recv):
    me = lax.axis_index("lat")
    count = lax.axis_size("lat")
    odd = me % 2
    even = 1 - odd
    fast = me + 1 - 2 * odd
    slow = me - 1 + 2 * odd
    has_slow = (slow >= 0) & (slow < count)
    target = {FAST: fast, SLOW: slow}
    token_count, width = atmos_in.shape
    groups = width // GROUP
    depth = width // scale_ref.shape[0]
    per_group = GROUP // depth
    key_pad = keys_wide.shape[0] // per_group
    och, orows, olon = ocean_in.shape
    wide = xs.shape[1]
    tiles = wide // 128
    nflux = wflux_ref.shape[0]
    taps, _, hid = first_in.shape
    opad = w_second.shape[0]
    alon = olon // SPAN
    tail = wide - 128
    first_pad = olon - tail
    total_rows = count * orows
    bf16 = jnp.bfloat16
    f32 = jnp.float32

    def send(kind, side, source, dest):
        return pltpu.make_async_remote_copy(
            src_ref=source, dst_ref=dest, send_sem=send_sems.at[kind, side],
            recv_sem=recv_sems.at[kind, side], device_id={"lat": target[side]},
            device_id_type=pl.DeviceIdType.MESH,
        )

    def start_both(kind, source, dest):
        send(kind, FAST, source, dest(FAST)).start()

        @pl.when(has_slow)
        def _():
            send(kind, SLOW, source, dest(SLOW)).start()

    def wait_both(kind, source, dest):
        send(kind, FAST, source, dest(FAST)).wait()

        @pl.when(has_slow)
        def _():
            send(kind, SLOW, source, dest(SLOW)).wait()

    def local_row(place):
        return odd * (place - orows) + even * (2 * orows - 1 - place)

    half_width = qkv_hbm.shape[1] // 2
    loads = (
        pltpu.make_async_copy(ocean_hbm, ocean_in, load_sems.at[0]),
        pltpu.make_async_copy(atmos_hbm, atmos_in, load_sems.at[1]),
        pltpu.make_async_copy(qkv_hbm.at[:, 0:half_width], hs.at[0:width, :], load_sems.at[2]),
        pltpu.make_async_copy(
            qkv_hbm.at[:, half_width:], hs.at[width : 2 * width, :], load_sems.at[3]),
        pltpu.make_async_copy(wout_hbm, hs.at[2 * width : 3 * width, 0:width], load_sems.at[4]),
        pltpu.make_async_copy(first_hbm, first_in, load_sems.at[5]),
        pltpu.make_async_copy(second_hbm, second_in, load_sems.at[6]),
    )
    for load in loads:
        load.start()
    barrier = pltpu.get_barrier_semaphore()
    pl.semaphore_signal(
        barrier, inc=1, device_id={"lat": fast}, device_id_type=pl.DeviceIdType.MESH)

    @pl.when(has_slow)
    def _():
        pl.semaphore_signal(
            barrier, inc=1, device_id={"lat": slow}, device_id_type=pl.DeviceIdType.MESH)

    @pl.when(jnp.logical_not(has_slow))
    def _():
        surf[SLOW] = jnp.zeros_like(surf[SLOW])
        rows[SLOW] = jnp.zeros_like(rows[SLOW])
        mid[SLOW] = jnp.zeros_like(mid[SLOW])
        land[SLOW] = jnp.zeros_like(land[SLOW])
        for i in range(orows):
            base = (2 * orows + i) * 3 * opad + opad
            xs[base : base + opad, :] = jnp.zeros((opad, wide), bf16)

    spans = lax.broadcasted_iota(jnp.int32, (olon, alon), 0) // SPAN
    chosen = spans == lax.broadcasted_iota(jnp.int32, (olon, alon), 1)
    mean = jnp.where(chosen, 1.0, 0.0).astype(bf16)
    loads[0].wait()
    top = jnp.concatenate(
        [ocean_in[v * LEVELS].astype(f32) for v in range(VARS)], axis=0).astype(bf16)
    surf[OWN] = (jnp.dot(top, mean, preferred_element_type=f32) * (1.0 / SPAN)).astype(bf16)
    land[OWN] = land_ref[...]
    pl.semaphore_wait(barrier, 1 + jnp.where(has_slow, 1, 0))

    def surf_at(side):
        return surf.at[side]

    def land_at(side):
        return land.at[side]

    start_both(0, surf.at[OWN], surf_at)
    start_both(1, land_ref, land_at)

    for c in range(opad):
        if c < och:
            cells = jnp.concatenate(
                [ocean_in[c].astype(f32), jnp.zeros((orows, wide - olon), f32)], axis=1)
        else:
            cells = jnp.zeros((orows, wide), f32)
        for t in range(tiles):
            line[pl.ds(t * orows * opad + c, orows, stride=opad), :] = cells[
                :, t * 128 : (t + 1) * 128]
    for place in range(orows, 2 * orows):
        base = place * 3 * opad + opad
        for t in range(tiles):
            at = pl.multiple_of(t * orows * opad + local_row(place) * opad, 16)
            xs[base : base + opad, t * 128 : (t + 1) * 128] = line[pl.ds(at, opad), :].astype(bf16)

    loads[5].wait()
    loads[6].wait()
    turned[...] = jnp.zeros_like(turned)
    row_id = lax.broadcasted_iota(jnp.int32, (opad, hid), 0)
    for k in range(taps):
        source = (odd * (k // 3) + even * (2 - k // 3)) * 3 + k % 3
        tap = first_in[source].astype(f32)
        turned[k * opad : (k + 1) * opad, :] = jnp.where(row_id < och, tap[0:opad], 0.0)
    w_state[...] = turned[...].T.astype(bf16)
    turned[...] = jnp.zeros_like(turned)
    for k in range(taps):
        source = (odd * (k // 3) + even * (2 - k // 3)) * 3 + k % 3
        turned[k * nflux : (k + 1) * nflux, :] = first_in[source].astype(f32)[och:]
        w_second[0:och, k * hid : (k + 1) * hid] = second_in[source]
        w_second[och:, k * hid : (k + 1) * hid] = jnp.zeros((opad - och, hid), bf16)
    w_flux[...] = turned[0 : w_flux.shape[1], :].T.astype(bf16)

    embed = jnp.concatenate(
        [jnp.broadcast_to(embed_ref[v : v + 1, :], (orows, width)) for v in range(VARS)], axis=0)
    which = lax.broadcasted_iota(jnp.int32, (VARS * orows, 1), 0) % orows
    scaled = []
    for device in (fast, me, slow):
        weights = jnp.zeros((VARS * orows, 1), f32)
        for i in range(orows):
            column = device * orows + i
            weight = jnp.float32(0.0)
            for b in range(surf_weight.shape[1]):
                weight = weight + jnp.where(surf_first[0] + b == column, surf_weight[0, b], 0.0)
            weight = jnp.where((column >= 0) & (column < total_rows), weight, 0.0)
            weights = jnp.where(which == i, weight, weights)
        scaled.append(weights * embed)
    scaled = jnp.concatenate(scaled, axis=0)
    high = scaled.astype(bf16)
    rest = scaled - high.astype(f32)
    middle = rest.astype(bf16)
    low = (rest - middle.astype(f32)).astype(bf16)
    scaled = jnp.concatenate([high, middle, low], axis=0)
    loads[1].wait()
    wait_both(0, surf.at[OWN], surf_at)
    fields = jnp.concatenate([surf[FAST], surf[OWN], surf[SLOW]], axis=0)
    fields = jnp.concatenate([fields] * 3, axis=0)
    started = atmos_in[...].astype(f32) + lax.dot_general(
        fields, scaled, (((0,), (0,)), ((), ())), preferred_element_type=f32)
    held = kept.at[0:token_count, 0:width]
    held[...] = started
    near[0] = rms_norm(started, gain_ref[...]).astype(bf16)

    @pl.when(has_slow)
    def _():
        send(2, SLOW, near.at[0], near.at[1]).start()

    lane = lax.broadcasted_iota(jnp.int32, (1, GROUP), 1) // depth
    half_lane = lax.broadcasted_iota(jnp.int32, (1, 128), 1) // depth
    stat_lane = lax.broadcasted_iota(jnp.int32, (1, 128), 1)

    def head_scales(raw):
        pieces = []
        for t in range(GROUP // 128):
            piece = raw[:, t * 128 : (t + 1) * 128]
            squares = piece * piece
            factor = jnp.zeros_like(piece)
            for h in range(128 // depth):
                total = jnp.sum(jnp.where(half_lane == h, squares, 0.0), axis=1, keepdims=True)
                factor = jnp.where(
                    half_lane == h, lax.rsqrt(total * (1.0 / depth) + 1e-06), factor)
            pieces.append(piece * factor)
        return jnp.concatenate(pieces, axis=1)

    def project(part, column):
        at = pl.ds(pl.multiple_of((column // half_width) * width, width), width)
        columns = pl.ds(pl.multiple_of(column % half_width, GROUP), GROUP)
        return jnp.dot(near[part], hs[at, columns], preferred_element_type=f32)

    per_tile = 128 // depth
    gathered = kept.at[token_count : 2 * token_count, 0:width]

    beyond = stat_lane + (key_pad - 128) >= token_count

    def attend(g, key, value, fresh):
        for h in range(per_group):
            columns = slice(h // per_tile * 128, (h // per_tile + 1) * 128)
            at = slice(h * key_pad, h * key_pad + token_count)
            mine = half_lane == h % per_tile
            keys_wide[at, :] = jnp.where(mine, key[:, columns], jnp.zeros((1, 128), bf16))
            vals_wide[at, :] = jnp.where(mine, value[:, columns], jnp.zeros((1, 128), bf16))
        for t in range(per_group // per_tile):
            both = slice(t * per_tile * key_pad, (t + 1) * per_tile * key_pad)
            scores = lax.dot_general(
                queries[g, :, t * 128 : (t + 1) * 128], keys_wide[both, :],
                (((1,), (1,)), ((), ())), preferred_element_type=f32)
            fade = None
            for j in range(per_tile):
                h = t * per_tile + j
                at = g * per_group + h
                base = j * key_pad
                pieces = [scores[:, base + i : base + i + 128] for i in range(0, key_pad, 128)]
                pieces[-1] = jnp.where(beyond, -1e30, pieces[-1])
                largest = pieces[0]
                for piece in pieces[1:]:
                    largest = jnp.maximum(largest, piece)
                largest = jnp.broadcast_to(
                    jnp.max(largest, axis=1, keepdims=True), (token_count, 128))
                if not fresh:
                    before = largest_at[at]
                    largest = jnp.maximum(largest, before)
                raised = [jnp.exp(piece - largest) for piece in pieces]
                total = raised[0]
                for piece in raised[1:]:
                    total = total + piece
                if not fresh:
                    factor = jnp.exp(before - largest)
                    total = total + total_at[at] * factor
                    fade = factor if fade is None else jnp.where(half_lane == j, factor, fade)
                largest_at[at] = largest
                total_at[at] = total
                for i, piece in enumerate(raised):
                    start = h * key_pad + i * 128
                    probs[:, start : start + 128] = piece.astype(bf16)
            mixed = jnp.dot(probs[:, both], vals_wide[both, :], preferred_element_type=f32)
            columns = pl.ds(pl.multiple_of(g * GROUP + t * 128, 128), 128)
            if fresh:
                gathered[:, columns] = mixed
            else:
                gathered[:, columns] = gathered[:, columns] * fade + mixed

    def kv_copy(g, kind):
        ref = (keys, vals)[kind]
        return pltpu.make_async_remote_copy(
            src_ref=ref.at[0, g], dst_ref=ref.at[1, g], send_sem=kv_send.at[kind, g],
            recv_sem=kv_recv.at[kind, g], device_id={"lat": fast},
            device_id_type=pl.DeviceIdType.MESH,
        )

    def halo_copy(side, place):
        goal = {FAST: 2 * orows - 1, SLOW: 4 * orows - 1}[side] - place
        source = xs.at[pl.ds(place * 3 * opad + opad, opad), :]
        dest = xs.at[pl.ds(goal * 3 * opad + opad, opad), :]
        return pltpu.make_async_remote_copy(
            src_ref=source, dst_ref=dest, send_sem=halo_send.at[side, place - orows],
            recv_sem=halo_recv.at[side, place - orows], device_id={"lat": target[side]},
            device_id_type=pl.DeviceIdType.MESH,
        )

    keys_wide[...] = jnp.zeros_like(keys_wide)
    vals_wide[...] = jnp.zeros_like(vals_wide)

    def own(g, carry):
        column = g * GROUP
        query = head_scales(project(0, column))
        scale = jnp.zeros((1, GROUP), f32)
        for h in range(per_group):
            scale = jnp.where(lane == h, scale_ref[g * per_group + h], scale)
        queries[g] = (query * (scale * (1.0 / depth**0.5))).astype(bf16)
        keys[0, g] = head_scales(project(0, width + column)).astype(bf16)
        vals[0, g] = project(0, 2 * width + column).astype(bf16)
        for kind in range(2):
            kv_copy(g, kind).start()
        attend(g, keys[0, g], vals[0, g], True)
        return carry

    loads[2].wait()
    loads[3].wait()
    lax.fori_loop(0, groups, own, 0)
    for place in range(orows, 2 * orows):
        halo_copy(FAST, place).start()

    def from_fast(g, carry):
        for kind in range(2):
            kv_copy(g, kind).wait()
        attend(g, keys[1, g], vals[1, g], False)
        return carry

    lax.fori_loop(0, groups, from_fast, 0)

    @pl.when(has_slow)
    def _():
        send(2, SLOW, near.at[0], near.at[1]).wait()
        for place in (2 * orows - 1, 2 * orows - 2):
            halo_copy(SLOW, place).start()

    def from_slow(g, carry):
        column = g * GROUP
        key = head_scales(project(1, width + column)).astype(bf16)
        value = project(1, 2 * width + column).astype(bf16)
        attend(g, key, value, False)
        return carry

    @pl.when(has_slow)
    def _():
        lax.fori_loop(0, groups, from_slow, 0)

    loads[4].wait()

    def finish(g, carry):
        columns = pl.ds(pl.multiple_of(g * GROUP, GROUP), GROUP)
        factors = []
        for t in range(per_group // per_tile):
            factor = None
            for j in range(per_tile):
                total = jnp.sum(total_at[g * per_group + t * per_tile + j], axis=1, keepdims=True)
                inverse = jnp.broadcast_to(1.0 / total, (token_count, 128))
                factor = inverse if factor is None else jnp.where(half_lane == j, inverse, factor)
            factors.append(factor)
        factor = jnp.concatenate(factors, axis=1)
        mixed = (gathered[:, columns] * factor).astype(bf16)
        at = pl.ds(pl.multiple_of(2 * width + g * GROUP, GROUP), GROUP)
        held[...] += jnp.dot(mixed, hs[at, 0:width], preferred_element_type=f32)
        return carry

    lax.fori_loop(0, groups, finish, 0)
    after = held[...]
    after_ref[...] = after.astype(bf16)
    flux_in = rms_norm(after, flux_gain_ref[...]).astype(bf16)
    rows[OWN] = lax.dot_general(
        wflux_ref[...], flux_in, (((1,), (1,)), ((), ())), preferred_element_type=f32
    ).astype(bf16)

    def rows_at(side):
        return rows.at[side]

    start_both(3, rows.at[OWN], rows_at)

    @pl.when(has_slow)
    def _():
        for place in range(2 * orows - 3, orows - 1, -1):
            halo_copy(SLOW, place).start()

    def spread(ref, base, size):
        center = pl.ds(base + size, size)
        head = ref[center, 0:128]
        last = ref[center, tail:]
        at = lax.broadcasted_iota(jnp.int32, last.shape, 1)
        end = pltpu.roll(last, 128 - first_pad, 1)
        begin = pltpu.roll(head, first_pad, 1)
        last = jnp.where(at == first_pad, begin, jnp.where(at == 127, end, last))
        whole = jnp.concatenate([ref[center, 0:tail], last], axis=1)
        ref[pl.ds(base, size), :] = pltpu.roll(whole, 1, 1)
        ref[pl.ds(base + 2 * size, size), :] = pltpu.roll(whole, wide - 1, 1)

    def spread_state(place, carry):
        spread(xs, pl.multiple_of(place * 3 * opad, 16), opad)
        return carry

    def spread_hidden(place):
        spread(hs, pl.multiple_of((place + 1) * 3 * hid, 16), hid)

    wait_both(1, land_ref, land_at)
    for side, base in ((FAST, 0), (OWN, orows), (SLOW, 2 * orows)):
        for i in range(orows):
            place = base + i
            if side == OWN:
                at = local_row(place)
            else:
                at = odd * i + even * (orows - 1 - i)
            cells = land[side, pl.ds(at, 1), :].astype(f32)
            sea[place, :, 0:tail] = cells[:, 0:tail]
            sea[place, :, tail:] = jnp.concatenate(
                [cells[:, tail:], jnp.zeros((1, wide - olon), f32)], axis=1)
    for place in range(orows, 2 * orows):
        halo_copy(FAST, place).wait()

    @pl.when(has_slow)
    def _():
        for place in (2 * orows - 1, 2 * orows - 2):
            halo_copy(SLOW, place).wait()

    lax.fori_loop(0, 2 * orows + 2, spread_state, 0)

    def state_part(place, n):
        block = xs[pl.ds(pl.multiple_of((place - 1) * 3 * opad, 16), 9 * opad), n : n + CHUNK]
        return jnp.dot(w_state[:, 0 : 9 * opad], block, preferred_element_type=f32)

    def keep_state(place, carry):
        for n in range(0, wide, CHUNK):
            kept[pl.ds(pl.multiple_of((place - 1) * hid, 16), hid), n : n + CHUNK] = state_part(
                place, n)
        return carry

    lax.fori_loop(1, orows + 1, keep_state, 0, unroll=2)
    wait_both(3, rows.at[OWN], rows_at)
    sources = [rows[side].astype(f32) for side in range(3)]
    for i in range(orows):
        at = local_row(orows + i)
        regridded = jnp.zeros_like(sources[0])
        for side, device in ((FAST, fast), (OWN, me), (SLOW, slow)):
            weight = jnp.float32(0.0)
            for b in range(flux_weight.shape[1]):
                weight = weight + jnp.where(
                    flux_first[at] + b == device, flux_weight[at, b], 0.0)
            regridded = regridded + weight * sources[side]
        mid[OWN, i] = regridded.astype(bf16)

    def mid_at(side):
        return mid.at[side]

    start_both(4, mid.at[OWN], mid_at)
    lax.fori_loop(orows + 1, 2 * orows + 1, keep_state, 0, unroll=2)
    wait_both(4, mid.at[OWN], mid_at)
    column = lax.broadcasted_iota(jnp.int32, (alon, wide), 1)
    longitude = jnp.where(column < olon, column, jnp.where(column == olon, 0, olon - 1))
    chosen = longitude // SPAN == lax.broadcasted_iota(jnp.int32, (alon, wide), 0)
    repeat = jnp.where(chosen, 1.0, 0.0).astype(bf16)
    every = [mid[FAST, orows - 1 - i] for i in range(orows)]
    every += [mid[OWN, i] for i in range(orows)]
    every += [mid[SLOW, orows - 1 - i] for i in range(orows)]
    repeated = jnp.dot(
        jnp.concatenate(every, axis=0), repeat, preferred_element_type=f32).astype(bf16)
    for place in range(3 * orows):
        base = place * 3 * nflux
        whole = repeated[place * nflux : (place + 1) * nflux]
        fx[base + nflux : base + 2 * nflux, :] = whole
        fx[base : base + nflux, :] = pltpu.roll(whole, 1, 1)
        fx[base + 2 * nflux : base + 3 * nflux, :] = pltpu.roll(whole, wide - 1, 1)

    @pl.when(has_slow)
    def _():
        for place in range(2 * orows - 3, orows - 1, -1):
            halo_copy(SLOW, place).wait()

    lax.fori_loop(2 * orows + 2, 3 * orows, spread_state, 0)
    root = (2.0 / jnp.pi) ** 0.5

    def inside_of(place):
        row = me * orows + local_row(place)
        return (row >= 0) & (row < total_rows)

    for step in range(OSTEPS):
        edge = 1 + 2 * step

        def first(place, both):
            half = jnp.where(inside_of(place), 0.5, 0.0).astype(f32)
            at = pl.ds(pl.multiple_of((place - 1) * hid, 16), hid)
            for n in range(0, wide, CHUNK):
                if step == 0:
                    block = fx[
                        pl.ds(pl.multiple_of((place - 1) * 3 * nflux, 16), 9 * nflux), n : n + CHUNK]
                    share = jnp.dot(w_flux[...], block, preferred_element_type=f32)
                    full = share + (state_part(place, n) if both else kept[at, n : n + CHUNK])
                    kept[at, n : n + CHUNK] = share
                else:
                    full = kept[at, n : n + CHUNK] + state_part(place, n)
                bent = jnp.tanh(full * (root + (root * 0.044715) * (full * full)))
                half_full = full * half
                hidden = half_full + half_full * bent
                hs[pl.ds(pl.multiple_of((place + 1) * 3 * hid + hid, 16), hid), n : n + CHUNK] = (
                    hidden.astype(bf16))

        def firsts(pair, carry, both=False):
            place = edge + 2 * pair
            for i in (-2, -1):
                spread_hidden(place + i)
            for i in (0, 1):
                first(place + i, both)
            return carry

        pairs = (3 * orows - 2 * edge) // 2
        if step == 0:
            lax.fori_loop(0, pairs - 1, firsts, 0)
            firsts(pairs - 1, 0, True)
        else:
            lax.fori_loop(0, pairs, firsts, 0)
        for i in (-2, -1):
            spread_hidden(3 * orows - edge + i)

        def second(place):
            for n in range(0, wide, CHUNK):
                block = hs[pl.ds(pl.multiple_of(place * 3 * hid, 16), 9 * hid), n : n + CHUNK]
                full = jnp.dot(w_second[...], block, preferred_element_type=f32)
                center = pl.ds(pl.multiple_of(place * 3 * opad + opad, 16), opad)
                if step == 0:
                    before = xs[center, n : n + CHUNK].astype(f32)
                else:
                    before = st[place - 2, :, n : n + CHUNK]
                state = before + sea[place, :, n : n + CHUNK] * full
                if step == OSTEPS - 1:
                    for t in range(CHUNK // 128):
                        at = (n // 128 + t) * orows * opad + local_row(place) * opad
                        line[pl.ds(pl.multiple_of(at, 16), opad), :] = state[
                            :, t * 128 : (t + 1) * 128]
                else:
                    st[place - 2, :, n : n + CHUNK] = state
                    xs[center, n : n + CHUNK] = state.astype(bf16)

        def seconds(pair, carry):
            place = edge + 1 + 2 * pair
            if step < OSTEPS - 1:
                for i in (-2, -1):
                    spread_state(place + i, 0)
            for i in (0, 1):
                second(place + i)
            return carry

        lax.fori_loop(0, (3 * orows - 2 * edge - 2) // 2, seconds, 0)
        if step < OSTEPS - 1:
            for i in (-2, -1):
                spread_state(3 * orows - edge - 1 + i, 0)

    for c in range(och):
        cells = jnp.concatenate(
            [line[pl.ds(t * orows * opad + c, orows, stride=opad), :] for t in range(tiles)], axis=1)
        out_ref[c] = cells[:, 0:olon].astype(bf16)


def local(
    atmos,
    ocean_state,
    land_mask,
    w_qkv,
    w_out,
    head_scale,
    gain_attn,
    gain_flux,
    w_flux,
    surf_embed,
    flux_start,
    flux_weight,
    surf_start,
    surf_weight,
    conv_first,
    conv_second,
):
    token_count, width = atmos.shape
    och, orows, olon = ocean_state.shape
    alon = olon // SPAN
    nflux = w_flux.shape[1]
    taps, hid, _ = conv_first.shape
    groups = width // GROUP
    per_group = GROUP // (width // head_scale.shape[0])
    key_pad = round_up(token_count, 128)
    opad = round_up(och, 16)
    wide = round_up(olon + 2, CHUNK)
    places = 3 * orows
    bf16 = jnp.bfloat16
    f32 = jnp.float32
    vmem = pl.BlockSpec(memory_space=pltpu.VMEM)
    smem = pl.BlockSpec(memory_space=pltpu.SMEM)
    anywhere = pl.BlockSpec(memory_space=pl.ANY)
    turned_shape = (round_up(taps * opad, 128), hid)
    return pl.pallas_call(
        step_kernel,
        out_shape=[
            jax.ShapeDtypeStruct(atmos.shape, bf16),
            jax.ShapeDtypeStruct(ocean_state.shape, bf16),
        ],
        in_specs=[smem] * 5 + [vmem] * 5 + [anywhere] * 6,
        out_specs=[vmem] * 2,
        scratch_shapes=[
            pltpu.VMEM(ocean_state.shape, bf16),
            pltpu.VMEM(atmos.shape, bf16),
            pltpu.VMEM((taps, och + nflux, hid), bf16),
            pltpu.VMEM(conv_second.shape, bf16),
            pltpu.VMEM((3, VARS * orows, alon), bf16),
            pltpu.VMEM((2, token_count, width), bf16),
            pltpu.VMEM((groups, token_count, GROUP), bf16),
            pltpu.VMEM((2, groups, token_count, GROUP), bf16),
            pltpu.VMEM((2, groups, token_count, GROUP), bf16),
            pltpu.VMEM((per_group * key_pad, 128), bf16),
            pltpu.VMEM((per_group * key_pad, 128), bf16),
            pltpu.VMEM((token_count, per_group * key_pad), bf16),
            pltpu.VMEM((head_scale.shape[0], token_count, 128), f32),
            pltpu.VMEM((head_scale.shape[0], token_count, 128), f32),
            pltpu.VMEM((3, nflux, alon), bf16),
            pltpu.VMEM((3, orows, nflux, alon), bf16),
            pltpu.VMEM((3, orows, olon), jnp.int32),
            pltpu.VMEM((places, 1, wide), f32),
            pltpu.VMEM((wide // 128 * orows * opad, 128), f32),
            pltpu.VMEM((places * 3 * opad, wide), bf16),
            pltpu.VMEM((places * 3 * nflux, wide), bf16),
            pltpu.VMEM((places * 3 * hid, wide), bf16),
            pltpu.VMEM((places - 4, opad, wide), f32),
            pltpu.VMEM(((places - 2) * hid, wide), f32),
            pltpu.VMEM(turned_shape, f32),
            pltpu.VMEM((hid, turned_shape[0]), bf16),
            pltpu.VMEM((hid, taps * nflux), bf16),
            pltpu.VMEM((opad, taps * hid), bf16),
            pltpu.SemaphoreType.DMA((7,)),
            pltpu.SemaphoreType.DMA((5, 3)),
            pltpu.SemaphoreType.DMA((5, 3)),
            pltpu.SemaphoreType.DMA((2, groups)),
            pltpu.SemaphoreType.DMA((2, groups)),
            pltpu.SemaphoreType.DMA((3, orows)),
            pltpu.SemaphoreType.DMA((3, orows)),
        ],
        compiler_params=pltpu.CompilerParams(
            collective_id=0, has_side_effects=True, vmem_limit_bytes=63 * 1024 * 1024
        ),
        name="coupled_step",
    )(surf_start, surf_weight, flux_start, flux_weight, head_scale, land_mask, surf_embed,
      gain_attn[None, :], gain_flux[None, :], w_flux.T, atmos, ocean_state, w_qkv, w_out,
      conv_first.transpose(0, 2, 1), conv_second)


def solution(mesh):
    in_specs = (
        P(("ens", "lat"), None),
        P(None, ("ens", "lat"), None),
        P("lat", None),
        P(),
        P(),
        P(),
        P(),
        P(),
        P(),
        P(),
        P("lat"),
        P("lat", None),
        P("lat"),
        P("lat", None),
        P(),
        P(),
    )
    out_specs = (P(("ens", "lat"), None), P(None, ("ens", "lat"), None))
    return jax.shard_map(local, mesh=mesh, in_specs=in_specs, out_specs=out_specs, check_vma=False)
```

```python
import jax
import jax.numpy as jnp
from jax import lax
from jax.experimental import pallas as pl
from jax.experimental.pallas import tpu as pltpu
from jax.sharding import PartitionSpec as P

LEVELS = 19
VARS = 4
SPAN = 4
OSTEPS = 2
GROUP = 256
CHUNK = 512
FAST, OWN, SLOW = 0, 1, 2


def round_up(value, unit):
    return (value + unit - 1) // unit * unit


def rms_norm(values, scaling):
    return values * lax.rsqrt(jnp.mean(values * values, axis=-1, keepdims=True) + 1e-06) * scaling


def step_kernel(surf_first, surf_weight, flux_first, flux_weight, scale_ref, land_ref, embed_ref,
                gain_ref, flux_gain_ref, wflux_ref, atmos_hbm, ocean_hbm, qkv_hbm, wout_hbm,
                first_hbm, second_hbm,
                after_hbm, line_hbm,
                ocean_in, atmos_in, atmos_near, fields, factors, edge, first_in, second_in, surf, near, queries, keys, vals, keys_wide,
                vals_wide, probs, largest_at, gathered, repeat, rows, mid, land, sea,
                after_out, line, xs, fx, hs, st, kept, turned, w_state, w_flux, w_second,
                load_sems, out_sems, send_sems, recv_sems, kv_send, kv_recv, halo_send, halo_recv):
    me = lax.axis_index("lat")
    count = lax.axis_size("lat")
    odd = me % 2
    even = 1 - odd
    fast = me + 1 - 2 * odd
    slow = me - 1 + 2 * odd
    has_slow = (slow >= 0) & (slow < count)
    target = {FAST: fast, SLOW: slow}
    token_count, width = atmos_in.shape
    groups = width // GROUP
    depth = width // scale_ref.shape[0]
    per_group = GROUP // depth
    padded = near.shape[1]
    per_tile = 128 // depth
    key_pad = keys_wide.shape[1] // per_group
    och, orows, olon = ocean_in.shape
    wide = xs.shape[1]
    tiles = wide // 128
    nflux = wflux_ref.shape[0]
    taps, _, hid = first_in.shape
    opad = w_second.shape[0]
    alon = olon // SPAN
    tail = wide - 128
    first_pad = olon - tail
    total_rows = count * orows
    bf16 = jnp.bfloat16
    f32 = jnp.float32

    def send(kind, side, source, dest):
        return pltpu.make_async_remote_copy(
            src_ref=source, dst_ref=dest, send_sem=send_sems.at[kind, side],
            recv_sem=recv_sems.at[kind, side], device_id={"lat": target[side]},
            device_id_type=pl.DeviceIdType.MESH,
        )

    def start_both(kind, source, dest):
        send(kind, FAST, source, dest(FAST)).start()

        @pl.when(has_slow)
        def _():
            send(kind, SLOW, source, dest(SLOW)).start()

    def wait_both(kind, source, dest):
        send(kind, FAST, source, dest(FAST)).wait()

        @pl.when(has_slow)
        def _():
            send(kind, SLOW, source, dest(SLOW)).wait()

    def local_row(place):
        return odd * (place - orows) + even * (2 * orows - 1 - place)

    half_width = qkv_hbm.shape[1] // 2
    loads = (
        pltpu.make_async_copy(ocean_hbm, ocean_in, load_sems.at[0]),
        pltpu.make_async_copy(atmos_hbm, atmos_in, load_sems.at[1]),
        pltpu.make_async_copy(qkv_hbm.at[:, 0:half_width], hs.at[0:width, :], load_sems.at[2]),
        pltpu.make_async_copy(
            qkv_hbm.at[:, half_width:], hs.at[width : 2 * width, :], load_sems.at[3]),
        pltpu.make_async_copy(wout_hbm, hs.at[2 * width : 3 * width, 0:width], load_sems.at[4]),
        pltpu.make_async_copy(first_hbm, first_in, load_sems.at[5]),
        pltpu.make_async_copy(second_hbm, second_in, load_sems.at[6]),
    )
    for load in loads:
        load.start()
    barrier = pltpu.get_barrier_semaphore()
    pl.semaphore_signal(
        barrier, inc=1, device_id={"lat": fast}, device_id_type=pl.DeviceIdType.MESH)

    @pl.when(has_slow)
    def _():
        pl.semaphore_signal(
            barrier, inc=1, device_id={"lat": slow}, device_id_type=pl.DeviceIdType.MESH)

    @pl.when(jnp.logical_not(has_slow))
    def _():
        surf[SLOW] = jnp.zeros_like(surf[SLOW])
        rows[SLOW] = jnp.zeros_like(rows[SLOW])
        mid[SLOW] = jnp.zeros_like(mid[SLOW])
        land[SLOW] = jnp.zeros_like(land[SLOW])
        for i in range(orows):
            base = (2 * orows + i) * 3 * opad + opad
            xs[base : base + opad, :] = jnp.zeros((opad, wide), bf16)

    column = lax.broadcasted_iota(jnp.int32, (alon, wide), 1)
    longitude = jnp.where(column < olon, column, jnp.where(column == olon, 0, olon - 1))
    first_column = lax.broadcasted_iota(jnp.int32, (alon, wide), 0) * SPAN
    chosen = (longitude >= first_column) & (longitude < first_column + SPAN)
    repeat[...] = jnp.where(chosen, 1.0, 0.0).astype(bf16)
    loads[0].wait()
    top = jnp.concatenate(
        [ocean_in[v * LEVELS].astype(f32) for v in range(VARS)], axis=0).astype(bf16)
    summed = lax.dot_general(
        top, repeat[:, 0:olon], (((1,), (1,)), ((), ())), preferred_element_type=f32)
    surf[OWN] = (summed * (1.0 / SPAN)).astype(bf16)
    land[OWN] = land_ref[...]
    pl.semaphore_wait(barrier, 1 + jnp.where(has_slow, 1, 0))

    def surf_at(side):
        return surf.at[side]

    def land_at(side):
        return land.at[side]

    start_both(0, surf.at[OWN], surf_at)

    @pl.when(has_slow)
    def _():
        send(2, SLOW, atmos_hbm, atmos_near).start()

    start_both(1, land_ref, land_at)

    for c in range(opad):
        if c < och:
            cells = jnp.concatenate(
                [ocean_in[c].astype(f32), jnp.zeros((orows, wide - olon), f32)], axis=1)
        else:
            cells = jnp.zeros((orows, wide), f32)
        for t in range(tiles):
            line[t, pl.ds(c, orows, stride=opad), :] = cells[
                :, t * 128 : (t + 1) * 128]
    for place in range(orows, 2 * orows):
        base = place * 3 * opad + opad
        for t in range(tiles):
            at = pl.multiple_of(local_row(place) * opad, 16)
            xs[base : base + opad, t * 128 : (t + 1) * 128] = line[t, pl.ds(at, opad), :].astype(bf16)
        if place < 2 * orows - 2:
            edge[place - orows] = xs[base : base + opad, :]

    def spread(ref, base, size):
        center = pl.ds(base + size, size)
        head = ref[center, 0:128]
        last = ref[center, tail:]
        at = lax.broadcasted_iota(jnp.int32, last.shape, 1)
        end = pltpu.roll(last, 128 - first_pad, 1)
        begin = pltpu.roll(head, first_pad, 1)
        last = jnp.where(at == first_pad, begin, jnp.where(at == 127, end, last))
        whole = jnp.concatenate([ref[center, 0:tail], last], axis=1)
        ref[pl.ds(base, size), :] = pltpu.roll(whole, 1, 1)
        ref[pl.ds(base + 2 * size, size), :] = pltpu.roll(whole, wide - 1, 1)

    def spread_state(place, carry):
        spread(xs, pl.multiple_of(place * 3 * opad, 16), opad)
        return carry

    def spread_hidden(place):
        spread(hs, pl.multiple_of((place + 1) * 3 * hid, 16), hid)

    lane = lax.broadcasted_iota(jnp.int32, (1, GROUP), 1) // depth
    half_lane = lax.broadcasted_iota(jnp.int32, (1, 128), 1) // depth
    stat_lane = lax.broadcasted_iota(jnp.int32, (1, 128), 1)

    keys_wide[...] = jnp.zeros_like(keys_wide)
    vals_wide[...] = jnp.zeros_like(vals_wide)
    for h in range(per_group):
        counted = jnp.where(half_lane == h % per_tile, 1.0, 0.0).astype(bf16)
        for slot in range(2):
            vals_wide[slot, h * key_pad : h * key_pad + padded, 128:] = jnp.broadcast_to(
                counted, (padded, 128))

    lax.fori_loop(orows, 2 * orows, spread_state, 0)

    loads[5].wait()
    loads[6].wait()
    turned[...] = jnp.zeros_like(turned)
    row_id = lax.broadcasted_iota(jnp.int32, (opad, hid), 0)
    for k in range(taps):
        source = (odd * (k // 3) + even * (2 - k // 3)) * 3 + k % 3
        tap = first_in[source].astype(f32)
        turned[k * opad : (k + 1) * opad, :] = jnp.where(row_id < och, tap[0:opad], 0.0)
    w_state[...] = turned[...].T.astype(bf16)
    turned[...] = jnp.zeros_like(turned)
    for k in range(taps):
        source = (odd * (k // 3) + even * (2 - k // 3)) * 3 + k % 3
        turned[k * nflux : (k + 1) * nflux, :] = first_in[source].astype(f32)[och:]
        w_second[0:och, k * hid : (k + 1) * hid] = second_in[source]
        w_second[och:, k * hid : (k + 1) * hid] = jnp.zeros((opad - och, hid), bf16)
    w_flux[...] = turned[0 : w_flux.shape[1], :].T.astype(bf16)

    embed = jnp.concatenate(
        [jnp.broadcast_to(embed_ref[v : v + 1, :], (orows, width)) for v in range(VARS)], axis=0)
    which = lax.broadcasted_iota(jnp.int32, (VARS * orows, 128), 0) % orows
    for part, device in enumerate((fast, me, slow)):
        weights = jnp.zeros((VARS * orows, 128), f32)
        for i in range(orows):
            column = device * orows + i
            weight = jnp.float32(0.0)
            for b in range(surf_weight.shape[1]):
                weight = weight + jnp.where(surf_first[0] + b == column, surf_weight[0, b], 0.0)
            weight = jnp.where((column >= 0) & (column < total_rows), weight, 0.0)
            weights = jnp.where(which == i, weight, weights)
        factors[0, part * VARS * orows : (part + 1) * VARS * orows, :] = weights

    def start_of(tokens, whose):
        scaled = factors[whose, :, 0:1] * jnp.concatenate([embed] * 3, axis=0)
        high = scaled.astype(bf16)
        rest = scaled - high.astype(f32)
        middle = rest.astype(bf16)
        low = (rest - middle.astype(f32)).astype(bf16)
        started = tokens[...].astype(f32) + lax.dot_general(
            jnp.concatenate([fields[whose]] * 3, axis=0),
            jnp.concatenate([high, middle, low], axis=0),
            (((0,), (0,)), ((), ())), preferred_element_type=f32)
        return jnp.concatenate([started, jnp.zeros((padded - token_count, width), f32)], axis=0)

    loads[1].wait()
    wait_both(0, surf.at[OWN], surf_at)
    fields[0] = jnp.concatenate([surf[FAST], surf[OWN], surf[SLOW]], axis=0)
    started = start_of(atmos_in, 0)
    held = kept.at[0:padded, 0:width]
    held[...] = started
    near[0] = rms_norm(started, gain_ref[...]).astype(bf16)

    def halo_copy(side, place):
        goal = {FAST: 2 * orows - 1, SLOW: 4 * orows - 1}[side] - place
        source = xs.at[pl.ds(place * 3 * opad + opad, opad), :]
        if side == SLOW and place < 2 * orows - 2:
            source = edge.at[place - orows]
        dest = xs.at[pl.ds(goal * 3 * opad + opad, opad), :]
        return pltpu.make_async_remote_copy(
            src_ref=source, dst_ref=dest, send_sem=halo_send.at[side, place - orows],
            recv_sem=halo_recv.at[side, place - orows], device_id={"lat": target[side]},
            device_id_type=pl.DeviceIdType.MESH,
        )

    @pl.when(has_slow)
    def _():
        send(5, SLOW, fields.at[0], fields.at[1]).start()
        send(6, SLOW, factors.at[0], factors.at[1]).start()

    middle_row = round_up(padded // 2, 16)
    blocks = (slice(0, middle_row), slice(middle_row, padded))
    ones_at = lax.broadcasted_iota(jnp.int32, (GROUP, 128), 0) % 128 // depth
    ones = jnp.where(ones_at == half_lane, 1.0, 0.0).astype(bf16)

    def head_scales(raw):
        pieces = []
        for t in range(GROUP // 128):
            piece = raw[:, t * 128 : (t + 1) * 128]
            squares = piece * piece
            coarse = squares.astype(bf16)
            fine = (squares - coarse.astype(f32)).astype(bf16)
            total = jnp.dot(
                jnp.concatenate([coarse, fine], axis=1), ones, preferred_element_type=f32)
            pieces.append(piece * lax.rsqrt(total * (1.0 / depth) + 1e-06))
        return jnp.concatenate(pieces, axis=1)

    def project(part, column, block):
        at = pl.ds(pl.multiple_of((column // half_width) * width, width), width)
        columns = pl.ds(pl.multiple_of(column % half_width, GROUP), GROUP)
        return jnp.dot(near[part, block, :], hs[at, columns], preferred_element_type=f32)

    beyond = stat_lane + (key_pad - 128) >= token_count

    def attend(g, key, value, fresh, slot):
        for h in range(per_group):
            columns = slice(h // per_tile * 128, (h // per_tile + 1) * 128)
            at = slice(h * key_pad, h * key_pad + padded)
            mine = half_lane == h % per_tile
            keys_wide[slot, at, :] = jnp.where(mine, key[:, columns], jnp.zeros((1, 128), bf16))
            vals_wide[slot, at, 0:128] = jnp.where(
                mine, value[:, columns], jnp.zeros((1, 128), bf16))
        for t in range(per_group // per_tile):
            both = slice(t * per_tile * key_pad, (t + 1) * per_tile * key_pad)
            where = g * (per_group // per_tile) + t
            for block in blocks:
                size = block.stop - block.start
                scores = lax.dot_general(
                    queries[g, block, t * 128 : (t + 1) * 128], keys_wide[slot, both, :],
                    (((1,), (1,)), ((), ())), preferred_element_type=f32)
                fade = None
                raised = []
                for j in range(per_tile):
                    at = g * per_group + t * per_tile + j
                    base = j * key_pad
                    pieces = [scores[:, base + i : base + i + 128] for i in range(0, key_pad, 128)]
                    pieces[-1] = jnp.where(beyond, -1e30, pieces[-1])
                    largest = pieces[0]
                    for piece in pieces[1:]:
                        largest = jnp.maximum(largest, piece)
                    largest = jnp.broadcast_to(jnp.max(largest, axis=1, keepdims=True), (size, 128))
                    if not fresh:
                        before = largest_at[at, block, :]
                        largest = jnp.maximum(largest, before)
                        factor = jnp.exp(before - largest)
                        fade = factor if fade is None else jnp.where(half_lane == j, factor, fade)
                    largest_at[at, block, :] = largest
                    raised += [jnp.exp(piece - largest) for piece in pieces]
                probs[slot, block, both] = jnp.concatenate(raised, axis=1).astype(bf16)
                mixed = jnp.dot(
                    probs[slot, block, both], vals_wide[slot, both, :], preferred_element_type=f32)
                if fresh:
                    gathered[where, block, :] = mixed
                else:
                    gathered[where, block, 0:128] = (
                        gathered[where, block, 0:128] * fade + mixed[:, 0:128])
                    gathered[where, block, 128:] = (
                        gathered[where, block, 128:] * fade + mixed[:, 128:])

    def kv_copy(g, kind):
        ref = (keys, vals)[kind]
        return pltpu.make_async_remote_copy(
            src_ref=ref.at[0, g], dst_ref=ref.at[1, g], send_sem=kv_send.at[kind, g],
            recv_sem=kv_recv.at[kind, g], device_id={"lat": fast},
            device_id_type=pl.DeviceIdType.MESH,
        )

    def by_two(body):
        def run(i, carry):
            for slot in range(2):
                body(2 * i + slot, slot)
            return carry
        lax.fori_loop(0, groups // 2, run, 0)

    def own(g, slot):
        column = g * GROUP
        scale = jnp.zeros((1, GROUP), f32)
        for h in range(per_group):
            scale = jnp.where(lane == h, scale_ref[g * per_group + h], scale)
        for block in blocks:
            query = head_scales(project(0, column, block))
            queries[g, block, :] = (query * (scale * (1.0 / depth**0.5))).astype(bf16)
            keys[0, g, block, :] = head_scales(project(0, width + column, block)).astype(bf16)
            vals[0, g, block, :] = project(0, 2 * width + column, block).astype(bf16)
        for kind in range(2):
            kv_copy(g, kind).start()
        attend(g, keys[0, g], vals[0, g], True, slot)

    loads[2].wait()
    loads[3].wait()
    by_two(own)
    for place in range(orows, 2 * orows):
        halo_copy(FAST, place).start()

    def from_fast(g, slot):
        for kind in range(2):
            kv_copy(g, kind).wait()
        attend(g, keys[1, g], vals[1, g], False, slot)

    by_two(from_fast)

    @pl.when(has_slow)
    def _():
        send(2, SLOW, atmos_hbm, atmos_near).wait()
        send(5, SLOW, fields.at[0], fields.at[1]).wait()
        send(6, SLOW, factors.at[0], factors.at[1]).wait()
        for place in (2 * orows - 1, 2 * orows - 2):
            halo_copy(SLOW, place).start()
        near[1] = rms_norm(start_of(atmos_near, 1), gain_ref[...]).astype(bf16)

    def fast_rows(i, carry):
        halo_copy(FAST, orows + i).wait()
        return spread_state(orows - 1 - i, carry)

    def from_slow(g, slot):
        column = g * GROUP
        key = jnp.concatenate(
            [head_scales(project(1, width + column, block)) for block in blocks], axis=0).astype(bf16)
        value = jnp.concatenate(
            [project(1, 2 * width + column, block) for block in blocks], axis=0).astype(bf16)
        attend(g, key, value, False, slot)

    @pl.when(has_slow)
    def _():
        by_two(from_slow)

    lax.fori_loop(0, orows, fast_rows, 0)
    loads[4].wait()

    for t in range(width // 128):
        near[0, :, t * 128 : (t + 1) * 128] = (
            gathered[t, :, 0:128] * (1.0 / gathered[t, :, 128:])).astype(bf16)
    pieces = []
    for n in range(0, width, CHUNK):
        piece = held[:, n : n + CHUNK] + jnp.dot(
            near[0], hs[2 * width : 3 * width, n : n + CHUNK], preferred_element_type=f32)
        pieces.append(piece[0:token_count])
    after = jnp.concatenate(pieces, axis=1)
    after_out[...] = after.astype(bf16)
    after_copy = pltpu.make_async_copy(after_out, after_hbm, out_sems.at[orows])
    after_copy.start()
    flux_in = rms_norm(after, flux_gain_ref[...]).astype(bf16)
    rows[OWN] = lax.dot_general(
        wflux_ref[...], flux_in, (((1,), (1,)), ((), ())), preferred_element_type=f32
    ).astype(bf16)

    def rows_at(side):
        return rows.at[side]

    start_both(3, rows.at[OWN], rows_at)

    wait_both(1, land_ref, land_at)
    for side, base in ((FAST, 0), (OWN, orows), (SLOW, 2 * orows)):
        for i in range(orows):
            place = base + i
            if side == OWN:
                at = local_row(place)
            else:
                at = odd * i + even * (orows - 1 - i)
            cells = land[side, pl.ds(at, 1), :].astype(f32)
            sea[place, :, 0:tail] = cells[:, 0:tail]
            sea[place, :, tail:] = jnp.concatenate(
                [cells[:, tail:], jnp.zeros((1, wide - olon), f32)], axis=1)
    @pl.when(has_slow)
    def _():
        for place in (2 * orows - 1, 2 * orows - 2):
            halo_copy(SLOW, place).wait()

    def state_part(place, n):
        block = xs[pl.ds(pl.multiple_of((place - 1) * 3 * opad, 16), 9 * opad), n : n + CHUNK]
        return jnp.dot(w_state[:, 0 : 9 * opad], block, preferred_element_type=f32)

    def keep_state(place, carry):
        for n in range(0, wide, CHUNK):
            kept[pl.ds(pl.multiple_of((place - 1) * hid, 16), hid), n : n + CHUNK] = state_part(
                place, n)
        return carry

    def keep_first(i, carry):
        spread_state(2 * orows + i, 0)
        for j in range(2):
            keep_state(1 + 2 * i + j, 0)
        return carry

    lax.fori_loop(0, 2, keep_first, 0)
    wait_both(3, rows.at[OWN], rows_at)
    sources = [rows[side].astype(f32) for side in range(3)]
    for i in range(orows):
        at = local_row(orows + i)
        regridded = jnp.zeros_like(sources[0])
        for side, device in ((FAST, fast), (OWN, me), (SLOW, slow)):
            weight = jnp.float32(0.0)
            for b in range(flux_weight.shape[0]):
                weight = weight + jnp.where(
                    flux_first[at] + b == device, flux_weight[b, at], 0.0)
            regridded = regridded + weight * sources[side]
        mid[OWN, i] = regridded.astype(bf16)

    def mid_at(side):
        return mid.at[side]

    start_both(4, mid.at[OWN], mid_at)

    @pl.when(has_slow)
    def _():
        for place in range(2 * orows - 3, orows - 1, -1):
            halo_copy(SLOW, place).start()

    lax.fori_loop(orows + 1, 2 * orows + 1, keep_state, 0, unroll=2)
    wait_both(4, mid.at[OWN], mid_at)
    every = [mid[FAST, orows - 1 - i] for i in range(orows)]
    every += [mid[OWN, i] for i in range(orows)]
    every += [mid[SLOW, orows - 1 - i] for i in range(orows)]
    repeated = jnp.dot(
        jnp.concatenate(every, axis=0), repeat[...], preferred_element_type=f32).astype(bf16)
    for place in range(3 * orows):
        base = place * 3 * nflux
        whole = repeated[place * nflux : (place + 1) * nflux]
        fx[base + nflux : base + 2 * nflux, :] = whole
        fx[base : base + nflux, :] = pltpu.roll(whole, 1, 1)
        fx[base + 2 * nflux : base + 3 * nflux, :] = pltpu.roll(whole, wide - 1, 1)

    root = (2.0 / jnp.pi) ** 0.5

    def inside_of(place):
        row = me * orows + local_row(place)
        return (row >= 0) & (row < total_rows)

    def first(step, place, both=False):
        half = jnp.where(inside_of(place), 0.5, 0.0).astype(f32)
        at = pl.ds(pl.multiple_of((place - 1) * hid, 16), hid)
        for n in range(0, wide, CHUNK):
            if step == 0:
                block = fx[
                    pl.ds(pl.multiple_of((place - 1) * 3 * nflux, 16), 9 * nflux), n : n + CHUNK]
                share = jnp.dot(w_flux[...], block, preferred_element_type=f32)
                full = share + (state_part(place, n) if both else kept[at, n : n + CHUNK])
                kept[at, n : n + CHUNK] = share
            else:
                full = kept[at, n : n + CHUNK] + state_part(place, n)
            bent = jnp.tanh(full * (root + (root * 0.044715) * (full * full)))
            half_full = full * half
            hidden = half_full + half_full * bent
            hs[pl.ds(pl.multiple_of((place + 1) * 3 * hid + hid, 16), hid), n : n + CHUNK] = (
                hidden.astype(bf16))

    def second(step, place):
        for n in range(0, wide, CHUNK):
            block = hs[pl.ds(pl.multiple_of(place * 3 * hid, 16), 9 * hid), n : n + CHUNK]
            full = jnp.dot(w_second[...], block, preferred_element_type=f32)
            center = pl.ds(pl.multiple_of(place * 3 * opad + opad, 16), opad)
            if step == 0:
                before = xs[center, n : n + CHUNK].astype(f32)
            else:
                before = st[place - orows, :, n : n + CHUNK]
            state = before + sea[place, :, n : n + CHUNK] * full
            if step == OSTEPS - 1:
                for t in range(CHUNK // 128):
                    at = pl.ds(pl.multiple_of(local_row(place) * opad, 16), opad)
                    line[n // 128 + t, at, :] = state[
                        :, t * 128 : (t + 1) * 128]
            else:
                if orows <= place < 2 * orows:
                    st[place - orows, :, n : n + CHUNK] = state
                xs[center, n : n + CHUNK] = state.astype(bf16)

    last = 3 * orows - 3

    def first_one(k, carry):
        for i in range(2):
            spread_hidden(2 * k - 1 + i)
        for i in range(2):
            first(0, 1 + 2 * k + i)
        return carry

    def finished(place):
        at = pl.ds(pl.multiple_of(local_row(place) * opad, 16), opad)
        return pltpu.make_async_copy(
            line.at[:, at, :], line_hbm.at[:, at, :], out_sems.at[place - orows])

    lax.fori_loop(0, (last - 1) // 2, first_one, 0)
    for place in range(2, last - 1):
        if place < 4:
            spread_hidden(last - 4 + place)
        else:
            spread_state(place - 2, 0)
        second(0, place)
    for place in range(3, last - 2):
        if place < 5:
            spread_state(last - 6 + place, 0)
        else:
            spread_hidden(place - 2)
        first(1, place)

    @pl.when(has_slow)
    def _():
        for place in range(2 * orows - 3, orows - 1, -1):
            halo_copy(SLOW, place).wait()

    for place in (last + 1, last + 2):
        spread_state(place, 0)
    for place in (last - 4, last - 3):
        spread_hidden(place)
    for place in (last, last + 1):
        first(0, place, True)
    for place in (last, last + 1):
        spread_hidden(place)
    for place in range(orows, last - 3):
        second(1, place)
        finished(place).start()
    for place in (last - 1, last):
        second(0, place)
    for place in (last - 1, last):
        spread_state(place, 0)
    for place in (last - 2, last - 1):
        first(1, place)
    for place in (last - 2, last - 1):
        spread_hidden(place)
    for place in range(last - 3, last - 1):
        second(1, place)
        finished(place).start()
    for place in range(orows, last - 1):
        finished(place).wait()
    after_copy.wait()


def output_kernel(after_hbm, line_hbm, atmos_hbm, ocean_hbm, after, line, ocean, in_sems, out_sems):
    och, orows, olon = ocean.shape
    tiles = line.shape[0]
    opad = line.shape[1] // orows
    per_step = CHUNK // 128
    after_in = pltpu.make_async_copy(after_hbm, after, in_sems.at[tiles // per_step])
    after_out = pltpu.make_async_copy(after, atmos_hbm, out_sems.at[0])
    ocean_out = pltpu.make_async_copy(ocean, ocean_hbm, out_sems.at[1])
    ins = []
    for step in range(tiles // per_step):
        at = slice(step * per_step, (step + 1) * per_step)
        ins.append(pltpu.make_async_copy(line_hbm.at[at], line.at[at], in_sems.at[step]))
    for copy in ins:
        copy.start()
    after_in.start()
    for step in range(tiles // per_step):
        ins[step].wait()
        begin = step * CHUNK
        end = min(begin + CHUNK, olon)
        for c in range(och):
            cells = [
                line[step * per_step + t, pl.ds(c, orows, stride=opad), :] for t in range(per_step)]
            cells = jnp.concatenate(cells, axis=1)[:, 0 : end - begin]
            ocean[c, :, begin:end] = cells.astype(ocean.dtype)
    ocean_out.start()
    after_in.wait()
    after_out.start()
    ocean_out.wait()
    after_out.wait()


def local(
    atmos,
    ocean_state,
    land_mask,
    w_qkv,
    w_out,
    head_scale,
    gain_attn,
    gain_flux,
    w_flux,
    surf_embed,
    flux_start,
    flux_weight,
    surf_start,
    surf_weight,
    conv_first,
    conv_second,
):
    token_count, width = atmos.shape
    och, orows, olon = ocean_state.shape
    alon = olon // SPAN
    nflux = w_flux.shape[1]
    taps, hid, _ = conv_first.shape
    groups = width // GROUP
    per_group = GROUP // (width // head_scale.shape[0])
    padded = round_up(token_count, 16)
    key_pad = round_up(token_count, 128)
    opad = round_up(och, 16)
    wide = round_up(olon + 2, CHUNK)
    places = 3 * orows
    bf16 = jnp.bfloat16
    f32 = jnp.float32
    vmem = pl.BlockSpec(memory_space=pltpu.VMEM)
    smem = pl.BlockSpec(memory_space=pltpu.SMEM)
    anywhere = pl.BlockSpec(memory_space=pl.ANY)
    turned_shape = (round_up(taps * opad, 128), hid)
    after, line = pl.pallas_call(
        step_kernel,
        out_shape=[
            jax.ShapeDtypeStruct(atmos.shape, bf16),
            jax.ShapeDtypeStruct((wide // 128, orows * opad, 128), f32),
        ],
        in_specs=[smem] * 5 + [vmem] * 5 + [anywhere] * 6,
        out_specs=[anywhere] * 2,
        scratch_shapes=[
            pltpu.VMEM(ocean_state.shape, bf16),
            pltpu.VMEM(atmos.shape, bf16),
            pltpu.VMEM(atmos.shape, bf16),
            pltpu.VMEM((2, 3 * VARS * orows, alon), bf16),
            pltpu.VMEM((2, 3 * VARS * orows, 128), f32),
            pltpu.VMEM((orows - 2, opad, wide), bf16),
            pltpu.VMEM((taps, och + nflux, hid), bf16),
            pltpu.VMEM(conv_second.shape, bf16),
            pltpu.VMEM((3, VARS * orows, alon), bf16),
            pltpu.VMEM((2, padded, width), bf16),
            pltpu.VMEM((groups, padded, GROUP), bf16),
            pltpu.VMEM((2, groups, padded, GROUP), bf16),
            pltpu.VMEM((2, groups, padded, GROUP), bf16),
            pltpu.VMEM((2, per_group * key_pad, 128), bf16),
            pltpu.VMEM((2, per_group * key_pad, GROUP), bf16),
            pltpu.VMEM((2, padded, per_group * key_pad), bf16),
            pltpu.VMEM((head_scale.shape[0], padded, 128), f32),
            pltpu.VMEM((width // 128, padded, GROUP), f32),
            pltpu.VMEM((alon, wide), bf16),
            pltpu.VMEM((3, nflux, alon), bf16),
            pltpu.VMEM((3, orows, nflux, alon), bf16),
            pltpu.VMEM((3, orows, olon), jnp.int32),
            pltpu.VMEM((places, 1, wide), f32),
            pltpu.VMEM(atmos.shape, bf16),
            pltpu.VMEM((wide // 128, orows * opad, 128), f32),
            pltpu.VMEM((places * 3 * opad, wide), bf16),
            pltpu.VMEM((places * 3 * nflux, wide), bf16),
            pltpu.VMEM((places * 3 * hid, wide), bf16),
            pltpu.VMEM((orows, opad, wide), f32),
            pltpu.VMEM(((places - 2) * hid, wide), f32),
            pltpu.VMEM(turned_shape, f32),
            pltpu.VMEM((hid, turned_shape[0]), bf16),
            pltpu.VMEM((hid, taps * nflux), bf16),
            pltpu.VMEM((opad, taps * hid), bf16),
            pltpu.SemaphoreType.DMA((7,)),
            pltpu.SemaphoreType.DMA((orows + 1,)),
            pltpu.SemaphoreType.DMA((7, 3)),
            pltpu.SemaphoreType.DMA((7, 3)),
            pltpu.SemaphoreType.DMA((2, groups)),
            pltpu.SemaphoreType.DMA((2, groups)),
            pltpu.SemaphoreType.DMA((3, orows)),
            pltpu.SemaphoreType.DMA((3, orows)),
        ],
        compiler_params=pltpu.CompilerParams(
            collective_id=0, has_side_effects=True, vmem_limit_bytes=63 * 1024 * 1024
        ),
        name="coupled_step",
    )(surf_start, surf_weight, flux_start, flux_weight.T, head_scale, land_mask, surf_embed,
      gain_attn[None, :], gain_flux[None, :], w_flux.T, atmos, ocean_state, w_qkv, w_out,
      conv_first.transpose(0, 2, 1), conv_second)
    return pl.pallas_call(
        output_kernel,
        out_shape=[
            jax.ShapeDtypeStruct(atmos.shape, bf16),
            jax.ShapeDtypeStruct(ocean_state.shape, bf16),
        ],
        in_specs=[anywhere] * 2,
        out_specs=[anywhere] * 2,
        scratch_shapes=[
            pltpu.VMEM(atmos.shape, bf16),
            pltpu.VMEM(line.shape, f32),
            pltpu.VMEM(ocean_state.shape, bf16),
            pltpu.SemaphoreType.DMA((wide // CHUNK + 1,)),
            pltpu.SemaphoreType.DMA((2,)),
        ],
        name="outputs",
    )(after, line)


def solution(mesh):
    in_specs = (
        P(("ens", "lat"), None),
        P(None, ("ens", "lat"), None),
        P("lat", None),
        P(),
        P(),
        P(),
        P(),
        P(),
        P(),
        P(),
        P("lat"),
        P("lat", None),
        P("lat"),
        P("lat", None),
        P(),
        P(),
    )
    out_specs = (P(("ens", "lat"), None), P(None, ("ens", "lat"), None))
    return jax.shard_map(local, mesh=mesh, in_specs=in_specs, out_specs=out_specs, check_vma=False)
```

```python
import jax
import jax.numpy as jnp
from jax import lax
from jax.experimental import pallas as pl
from jax.experimental.pallas import tpu as pltpu
from jax.sharding import PartitionSpec as P

LEVELS = 19
VARS = 4
SPAN = 4
OSTEPS = 2
GROUP = 256
CHUNK = 512
FAST, OWN, SLOW = 0, 1, 2


def round_up(value, unit):
    return (value + unit - 1) // unit * unit


def rms_norm(values, scaling):
    return values * lax.rsqrt(jnp.mean(values * values, axis=-1, keepdims=True) + 1e-06) * scaling


def step_kernel(surf_first, surf_weight, flux_first, flux_weight, scale_ref, land_ref, embed_ref,
                gain_ref, flux_gain_ref, wflux_ref, atmos_hbm, ocean_hbm, qkv_hbm, wout_hbm,
                first_hbm, second_hbm,
                after_hbm, line_hbm,
                ocean_in, atmos_in, atmos_near, factors, edge, first_in, second_in, surf, near, queries, keys, vals, keys_wide,
                vals_wide, probs, largest_at, gathered, repeat, rows, mid, land, sea,
                after_out, line, xs, fx, hs, st, kept, turned, w_state, w_flux, w_second,
                load_sems, out_sems, send_sems, recv_sems, kv_send, kv_recv, halo_send, halo_recv):
    me = lax.axis_index("lat")
    count = lax.axis_size("lat")
    odd = me % 2
    even = 1 - odd
    fast = me + 1 - 2 * odd
    slow = me - 1 + 2 * odd
    has_slow = (slow >= 0) & (slow < count)
    target = {FAST: fast, SLOW: slow}
    token_count, width = atmos_in.shape
    groups = width // GROUP
    depth = width // scale_ref.shape[0]
    per_group = GROUP // depth
    padded = near.shape[1]
    per_tile = 128 // depth
    key_pad = keys_wide.shape[1] // per_group
    och, orows, olon = ocean_in.shape
    wide = xs.shape[1]
    tiles = wide // 128
    nflux = wflux_ref.shape[0]
    taps, _, hid = first_in.shape
    opad = w_second.shape[0]
    alon = olon // SPAN
    tail = wide - 128
    first_pad = olon - tail
    total_rows = count * orows
    band = surf_weight.shape[1]
    beyond_slow = slow - 1 + 2 * odd
    bf16 = jnp.bfloat16
    f32 = jnp.float32

    def send(kind, side, source, dest):
        return pltpu.make_async_remote_copy(
            src_ref=source, dst_ref=dest, send_sem=send_sems.at[kind, side],
            recv_sem=recv_sems.at[kind, side], device_id={"lat": target[side]},
            device_id_type=pl.DeviceIdType.MESH,
        )

    def start_both(kind, source, dest):
        send(kind, FAST, source, dest(FAST)).start()

        @pl.when(has_slow)
        def _():
            send(kind, SLOW, source, dest(SLOW)).start()

    def wait_both(kind, source, dest):
        send(kind, FAST, source, dest(FAST)).wait()

        @pl.when(has_slow)
        def _():
            send(kind, SLOW, source, dest(SLOW)).wait()

    def local_row(place):
        return odd * (place - orows) + even * (2 * orows - 1 - place)

    half_width = qkv_hbm.shape[1] // 2
    loads = (
        pltpu.make_async_copy(ocean_hbm, ocean_in, load_sems.at[0]),
        pltpu.make_async_copy(atmos_hbm, atmos_in, load_sems.at[1]),
        pltpu.make_async_copy(qkv_hbm.at[:, 0:half_width], hs.at[0:width, :], load_sems.at[2]),
        pltpu.make_async_copy(
            qkv_hbm.at[:, half_width:], hs.at[width : 2 * width, :], load_sems.at[3]),
        pltpu.make_async_copy(wout_hbm, hs.at[2 * width : 3 * width, 0:width], load_sems.at[4]),
        pltpu.make_async_copy(first_hbm, first_in, load_sems.at[5]),
        pltpu.make_async_copy(second_hbm, second_in, load_sems.at[6]),
    )
    for load in loads:
        load.start()
    barrier = pltpu.get_barrier_semaphore()
    pl.semaphore_signal(
        barrier, inc=1, device_id={"lat": fast}, device_id_type=pl.DeviceIdType.MESH)

    @pl.when(has_slow)
    def _():
        pl.semaphore_signal(
            barrier, inc=1, device_id={"lat": slow}, device_id_type=pl.DeviceIdType.MESH)

    @pl.when(jnp.logical_not(has_slow))
    def _():
        surf[SLOW] = jnp.zeros_like(surf[SLOW])
        rows[SLOW] = jnp.zeros_like(rows[SLOW])
        mid[SLOW] = jnp.zeros_like(mid[SLOW])
        land[SLOW] = jnp.zeros_like(land[SLOW])
        for i in range(orows):
            base = (2 * orows + i) * 3 * opad + opad
            xs[base : base + opad, :] = jnp.zeros((opad, wide), bf16)

    column = lax.broadcasted_iota(jnp.int32, (alon, wide), 1)
    longitude = jnp.where(column < olon, column, jnp.where(column == olon, 0, olon - 1))
    first_column = lax.broadcasted_iota(jnp.int32, (alon, wide), 0) * SPAN
    chosen = (longitude >= first_column) & (longitude < first_column + SPAN)
    repeat[...] = jnp.where(chosen, 1.0, 0.0).astype(bf16)
    row_at = lax.broadcasted_iota(jnp.int32, factors.shape[1:], 0)
    filled = jnp.where(row_at == band, surf_first[0].astype(f32), 0.0)
    for b in range(band):
        filled = jnp.where(row_at == b, surf_weight[0, b], filled)
    factors[0] = filled
    loads[0].wait()
    top = jnp.concatenate(
        [ocean_in[v * LEVELS].astype(f32) for v in range(VARS)], axis=0).astype(bf16)
    summed = lax.dot_general(
        top, repeat[:, 0:olon], (((1,), (1,)), ((), ())), preferred_element_type=f32)
    surf[OWN] = (summed * (1.0 / SPAN)).astype(bf16)
    land[OWN] = land_ref[...]
    pl.semaphore_wait(barrier, 1 + jnp.where(has_slow, 1, 0))

    def surf_at(side):
        return surf.at[side]

    def land_at(side):
        return land.at[side]

    start_both(0, surf.at[OWN], surf_at)

    @pl.when(has_slow)
    def _():
        send(6, SLOW, factors.at[0], factors.at[1]).start()

    start_both(1, land_ref, land_at)

    for c in range(opad):
        if c < och:
            cells = jnp.concatenate(
                [ocean_in[c].astype(f32), jnp.zeros((orows, wide - olon), f32)], axis=1)
        else:
            cells = jnp.zeros((orows, wide), f32)
        for t in range(tiles):
            line[t, pl.ds(c, orows, stride=opad), :] = cells[
                :, t * 128 : (t + 1) * 128]
    for place in range(orows, 2 * orows):
        base = place * 3 * opad + opad
        for t in range(tiles):
            at = pl.multiple_of(local_row(place) * opad, 16)
            xs[base : base + opad, t * 128 : (t + 1) * 128] = line[t, pl.ds(at, opad), :].astype(bf16)
        if place < 2 * orows - 2:
            edge[place - orows] = xs[base : base + opad, :]

    def spread(ref, base, size):
        center = pl.ds(base + size, size)
        head = ref[center, 0:128]
        last = ref[center, tail:]
        at = lax.broadcasted_iota(jnp.int32, last.shape, 1)
        end = pltpu.roll(last, 128 - first_pad, 1)
        begin = pltpu.roll(head, first_pad, 1)
        last = jnp.where(at == first_pad, begin, jnp.where(at == 127, end, last))
        whole = jnp.concatenate([ref[center, 0:tail], last], axis=1)
        ref[pl.ds(base, size), :] = pltpu.roll(whole, 1, 1)
        ref[pl.ds(base + 2 * size, size), :] = pltpu.roll(whole, wide - 1, 1)

    def spread_state(place, carry):
        spread(xs, pl.multiple_of(place * 3 * opad, 16), opad)
        return carry

    def spread_hidden(place):
        spread(hs, pl.multiple_of((place + 1) * 3 * hid, 16), hid)

    lane = lax.broadcasted_iota(jnp.int32, (1, GROUP), 1) // depth
    half_lane = lax.broadcasted_iota(jnp.int32, (1, 128), 1) // depth
    stat_lane = lax.broadcasted_iota(jnp.int32, (1, 128), 1)

    keys_wide[...] = jnp.zeros_like(keys_wide)
    vals_wide[...] = jnp.zeros_like(vals_wide)
    for h in range(per_group):
        counted = jnp.where(half_lane == h % per_tile, 1.0, 0.0).astype(bf16)
        for slot in range(2):
            vals_wide[slot, h * key_pad : h * key_pad + padded, 128:] = jnp.broadcast_to(
                counted, (padded, 128))

    lax.fori_loop(orows, 2 * orows, spread_state, 0)

    loads[5].wait()
    loads[6].wait()
    turned[...] = jnp.zeros_like(turned)
    row_id = lax.broadcasted_iota(jnp.int32, (opad, hid), 0)
    for k in range(taps):
        source = (odd * (k // 3) + even * (2 - k // 3)) * 3 + k % 3
        tap = first_in[source].astype(f32)
        turned[k * opad : (k + 1) * opad, :] = jnp.where(row_id < och, tap[0:opad], 0.0)
    w_state[...] = turned[...].T.astype(bf16)
    turned[...] = jnp.zeros_like(turned)
    for k in range(taps):
        source = (odd * (k // 3) + even * (2 - k // 3)) * 3 + k % 3
        turned[k * nflux : (k + 1) * nflux, :] = first_in[source].astype(f32)[och:]
        w_second[0:och, k * hid : (k + 1) * hid] = second_in[source]
        w_second[och:, k * hid : (k + 1) * hid] = jnp.zeros((opad - och, hid), bf16)
    w_flux[...] = turned[0 : w_flux.shape[1], :].T.astype(bf16)

    embed = jnp.concatenate(
        [jnp.broadcast_to(embed_ref[v : v + 1, :], (orows, width)) for v in range(VARS)], axis=0)
    which = lax.broadcasted_iota(jnp.int32, (VARS * orows, 128), 0) % orows

    def start_of(tokens, whose, parts, devices):
        starts = factors[whose, band : band + 1, :]
        scaled = []
        for device in devices:
            column = which + device * orows
            weights = jnp.zeros((VARS * orows, 128), f32)
            for b in range(band):
                weights = weights + jnp.where(
                    column.astype(f32) == starts + b, factors[whose, b : b + 1, :], 0.0)
            weights = jnp.where((column >= 0) & (column < total_rows), weights, 0.0)
            scaled.append(jnp.concatenate([weights] * (width // 128), axis=1) * embed)
        scaled = jnp.concatenate(scaled, axis=0)
        high = scaled.astype(bf16)
        rest = scaled - high.astype(f32)
        middle = rest.astype(bf16)
        low = (rest - middle.astype(f32)).astype(bf16)
        fields = jnp.concatenate([surf[part] for part in parts] * 3, axis=0)
        started = tokens[...].astype(f32) + lax.dot_general(
            fields, jnp.concatenate([high, middle, low], axis=0),
            (((0,), (0,)), ((), ())), preferred_element_type=f32)
        return jnp.concatenate([started, jnp.zeros((padded - token_count, width), f32)], axis=0)

    loads[1].wait()
    wait_both(0, surf.at[OWN], surf_at)

    @pl.when(has_slow)
    def _():
        send(2, SLOW, atmos_hbm, atmos_near).start()

    started = start_of(atmos_in, 0, (FAST, OWN, SLOW), (fast, me, slow))
    held = kept.at[0:padded, 0:width]
    held[...] = started
    near[0] = rms_norm(started, gain_ref[...]).astype(bf16)

    def halo_copy(side, place):
        goal = {FAST: 2 * orows - 1, SLOW: 4 * orows - 1}[side] - place
        source = xs.at[pl.ds(place * 3 * opad + opad, opad), :]
        if side == SLOW and place < 2 * orows - 2:
            source = edge.at[place - orows]
        dest = xs.at[pl.ds(goal * 3 * opad + opad, opad), :]
        return pltpu.make_async_remote_copy(
            src_ref=source, dst_ref=dest, send_sem=halo_send.at[side, place - orows],
            recv_sem=halo_recv.at[side, place - orows], device_id={"lat": target[side]},
            device_id_type=pl.DeviceIdType.MESH,
        )

    @pl.when(has_slow)
    def _():
        send(5, SLOW, surf.at[FAST], surf.at[3]).start()

    blocks = (slice(0, padded),)
    ones_at = lax.broadcasted_iota(jnp.int32, (GROUP, 128), 0) % 128 // depth
    ones = jnp.where(ones_at == half_lane, 1.0, 0.0).astype(bf16)

    def head_scales(raw):
        pieces = []
        for t in range(GROUP // 128):
            piece = raw[:, t * 128 : (t + 1) * 128]
            squares = piece * piece
            coarse = squares.astype(bf16)
            fine = (squares - coarse.astype(f32)).astype(bf16)
            total = jnp.dot(
                jnp.concatenate([coarse, fine], axis=1), ones, preferred_element_type=f32)
            pieces.append(piece * lax.rsqrt(total * (1.0 / depth) + 1e-06))
        return jnp.concatenate(pieces, axis=1)

    def project(part, column, block):
        at = pl.ds(pl.multiple_of((column // half_width) * width, width), width)
        columns = pl.ds(pl.multiple_of(column % half_width, GROUP), GROUP)
        return jnp.dot(near[part, block, :], hs[at, columns], preferred_element_type=f32)

    beyond = stat_lane + (key_pad - 128) >= token_count

    def attend(g, key, value, fresh, slot):
        for h in range(per_group):
            columns = slice(h // per_tile * 128, (h // per_tile + 1) * 128)
            at = slice(h * key_pad, h * key_pad + padded)
            mine = half_lane == h % per_tile
            keys_wide[slot, at, :] = jnp.where(mine, key[:, columns], jnp.zeros((1, 128), bf16))
            vals_wide[slot, at, 0:128] = jnp.where(
                mine, value[:, columns], jnp.zeros((1, 128), bf16))
        for t in range(per_group // per_tile):
            both = slice(t * per_tile * key_pad, (t + 1) * per_tile * key_pad)
            where = g * (per_group // per_tile) + t
            for block in blocks:
                size = block.stop - block.start
                scores = lax.dot_general(
                    queries[g, block, t * 128 : (t + 1) * 128], keys_wide[slot, both, :],
                    (((1,), (1,)), ((), ())), preferred_element_type=f32)
                fade = None
                raised = []
                for j in range(per_tile):
                    at = g * per_group + t * per_tile + j
                    base = j * key_pad
                    pieces = [scores[:, base + i : base + i + 128] for i in range(0, key_pad, 128)]
                    pieces[-1] = jnp.where(beyond, -1e30, pieces[-1])
                    largest = pieces[0]
                    for piece in pieces[1:]:
                        largest = jnp.maximum(largest, piece)
                    largest = jnp.broadcast_to(jnp.max(largest, axis=1, keepdims=True), (size, 128))
                    if not fresh:
                        before = largest_at[at, block, :]
                        largest = jnp.maximum(largest, before)
                        factor = jnp.exp(before - largest)
                        fade = factor if fade is None else jnp.where(half_lane == j, factor, fade)
                    largest_at[at, block, :] = largest
                    raised += [jnp.exp(piece - largest) for piece in pieces]
                probs[slot, block, both] = jnp.concatenate(raised, axis=1).astype(bf16)
                mixed = jnp.dot(
                    probs[slot, block, both], vals_wide[slot, both, :], preferred_element_type=f32)
                if fresh:
                    gathered[where, block, :] = mixed
                else:
                    gathered[where, block, 0:128] = (
                        gathered[where, block, 0:128] * fade + mixed[:, 0:128])
                    gathered[where, block, 128:] = (
                        gathered[where, block, 128:] * fade + mixed[:, 128:])

    def kv_copy(g, kind):
        ref = (keys, vals)[kind]
        return pltpu.make_async_remote_copy(
            src_ref=ref.at[0, g], dst_ref=ref.at[1, g], send_sem=kv_send.at[kind, g],
            recv_sem=kv_recv.at[kind, g], device_id={"lat": fast},
            device_id_type=pl.DeviceIdType.MESH,
        )

    def by_two(body):
        def run(i, carry):
            for slot in range(2):
                body(2 * i + slot, slot)
            return carry
        lax.fori_loop(0, groups // 2, run, 0)

    def own(g, slot):
        column = g * GROUP
        scale = jnp.zeros((1, GROUP), f32)
        for h in range(per_group):
            scale = jnp.where(lane == h, scale_ref[g * per_group + h], scale)
        for block in blocks:
            query = head_scales(project(0, column, block))
            queries[g, block, :] = (query * (scale * (1.0 / depth**0.5))).astype(bf16)
            keys[0, g, block, :] = head_scales(project(0, width + column, block)).astype(bf16)
            vals[0, g, block, :] = project(0, 2 * width + column, block).astype(bf16)
        for kind in range(2):
            kv_copy(g, kind).start()
        attend(g, keys[0, g], vals[0, g], True, slot)

    loads[2].wait()
    loads[3].wait()
    by_two(own)
    for place in range(orows, 2 * orows):
        halo_copy(FAST, place).start()

    def from_fast(g, slot):
        for kind in range(2):
            kv_copy(g, kind).wait()
        attend(g, keys[1, g], vals[1, g], False, slot)

    by_two(from_fast)

    @pl.when(has_slow)
    def _():
        send(2, SLOW, atmos_hbm, atmos_near).wait()
        send(5, SLOW, surf.at[FAST], surf.at[3]).wait()
        send(6, SLOW, factors.at[0], factors.at[1]).wait()
        for place in (2 * orows - 1, 2 * orows - 2):
            halo_copy(SLOW, place).start()
        near[1] = rms_norm(start_of(
            atmos_near, 1, (3, SLOW, OWN), (beyond_slow, slow, me)), gain_ref[...]).astype(bf16)

    def fast_rows(i, carry):
        halo_copy(FAST, orows + i).wait()
        return spread_state(orows - 1 - i, carry)

    def from_slow(g, slot):
        column = g * GROUP
        key = jnp.concatenate(
            [head_scales(project(1, width + column, block)) for block in blocks], axis=0).astype(bf16)
        value = jnp.concatenate(
            [project(1, 2 * width + column, block) for block in blocks], axis=0).astype(bf16)
        attend(g, key, value, False, slot)

    @pl.when(has_slow)
    def _():
        by_two(from_slow)

    lax.fori_loop(0, orows, fast_rows, 0)
    loads[4].wait()

    for t in range(width // 128):
        near[0, :, t * 128 : (t + 1) * 128] = (
            gathered[t, :, 0:128] * (1.0 / gathered[t, :, 128:])).astype(bf16)
    pieces = []
    for n in range(0, width, CHUNK):
        piece = held[:, n : n + CHUNK] + jnp.dot(
            near[0], hs[2 * width : 3 * width, n : n + CHUNK], preferred_element_type=f32)
        pieces.append(piece[0:token_count])
    after = jnp.concatenate(pieces, axis=1)
    after_out[...] = after.astype(bf16)
    after_copy = pltpu.make_async_copy(after_out, after_hbm, out_sems.at[orows])
    after_copy.start()
    flux_in = rms_norm(after, flux_gain_ref[...]).astype(bf16)
    rows[OWN] = lax.dot_general(
        wflux_ref[...], flux_in, (((1,), (1,)), ((), ())), preferred_element_type=f32
    ).astype(bf16)

    def rows_at(side):
        return rows.at[side]

    start_both(3, rows.at[OWN], rows_at)


    wait_both(1, land_ref, land_at)
    for side, base in ((FAST, 0), (OWN, orows), (SLOW, 2 * orows)):
        for i in range(orows):
            place = base + i
            if side == OWN:
                at = local_row(place)
            else:
                at = odd * i + even * (orows - 1 - i)
            cells = land[side, pl.ds(at, 1), :].astype(f32)
            sea[place, :, 0:tail] = cells[:, 0:tail]
            sea[place, :, tail:] = jnp.concatenate(
                [cells[:, tail:], jnp.zeros((1, wide - olon), f32)], axis=1)
    @pl.when(has_slow)
    def _():
        for place in (2 * orows - 1, 2 * orows - 2):
            halo_copy(SLOW, place).wait()

    def state_part(place, n):
        block = xs[pl.ds(pl.multiple_of((place - 1) * 3 * opad, 16), 9 * opad), n : n + CHUNK]
        return jnp.dot(w_state[:, 0 : 9 * opad], block, preferred_element_type=f32)

    def keep_state(place, carry):
        for n in range(0, wide, CHUNK):
            kept[pl.ds(pl.multiple_of((place - 1) * hid, 16), hid), n : n + CHUNK] = state_part(
                place, n)
        return carry

    def keep_first(i, carry):
        spread_state(2 * orows + i, 0)
        for j in range(2):
            keep_state(1 + 2 * i + j, 0)
        return carry

    lax.fori_loop(0, 2, keep_first, 0)
    wait_both(3, rows.at[OWN], rows_at)
    sources = [rows[side].astype(f32) for side in range(3)]
    for i in range(orows):
        at = local_row(orows + i)
        regridded = jnp.zeros_like(sources[0])
        for side, device in ((FAST, fast), (OWN, me), (SLOW, slow)):
            weight = jnp.float32(0.0)
            for b in range(flux_weight.shape[0]):
                weight = weight + jnp.where(
                    flux_first[at] + b == device, flux_weight[b, at], 0.0)
            regridded = regridded + weight * sources[side]
        mid[OWN, i] = regridded.astype(bf16)

    def mid_at(side):
        return mid.at[side]

    start_both(4, mid.at[OWN], mid_at)

    lax.fori_loop(orows + 1, 2 * orows + 1, keep_state, 0, unroll=2)
    wait_both(4, mid.at[OWN], mid_at)

    @pl.when(has_slow)
    def _():
        for place in range(2 * orows - 3, orows - 1, -1):
            halo_copy(SLOW, place).start()

    every = [mid[FAST, orows - 1 - i] for i in range(orows)]
    every += [mid[OWN, i] for i in range(orows)]
    every += [mid[SLOW, orows - 1 - i] for i in range(orows)]
    repeated = jnp.dot(
        jnp.concatenate(every, axis=0), repeat[...], preferred_element_type=f32).astype(bf16)
    for place in range(3 * orows):
        base = place * 3 * nflux
        whole = repeated[place * nflux : (place + 1) * nflux]
        fx[base + nflux : base + 2 * nflux, :] = whole
        fx[base : base + nflux, :] = pltpu.roll(whole, 1, 1)
        fx[base + 2 * nflux : base + 3 * nflux, :] = pltpu.roll(whole, wide - 1, 1)

    root = (2.0 / jnp.pi) ** 0.5

    def inside_of(place):
        row = me * orows + local_row(place)
        return (row >= 0) & (row < total_rows)

    def first(step, place, both=False):
        half = jnp.where(inside_of(place), 0.5, 0.0).astype(f32)
        at = pl.ds(pl.multiple_of((place - 1) * hid, 16), hid)
        for n in range(0, wide, CHUNK):
            if step == 0:
                block = fx[
                    pl.ds(pl.multiple_of((place - 1) * 3 * nflux, 16), 9 * nflux), n : n + CHUNK]
                share = jnp.dot(w_flux[...], block, preferred_element_type=f32)
                full = share + (state_part(place, n) if both else kept[at, n : n + CHUNK])
                kept[at, n : n + CHUNK] = share
            else:
                full = kept[at, n : n + CHUNK] + state_part(place, n)
            bent = jnp.tanh(full * (root + (root * 0.044715) * (full * full)))
            half_full = full * half
            hidden = half_full + half_full * bent
            hs[pl.ds(pl.multiple_of((place + 1) * 3 * hid + hid, 16), hid), n : n + CHUNK] = (
                hidden.astype(bf16))

    def second(step, place):
        for n in range(0, wide, CHUNK):
            block = hs[pl.ds(pl.multiple_of(place * 3 * hid, 16), 9 * hid), n : n + CHUNK]
            full = jnp.dot(w_second[...], block, preferred_element_type=f32)
            center = pl.ds(pl.multiple_of(place * 3 * opad + opad, 16), opad)
            if step == 0:
                before = xs[center, n : n + CHUNK].astype(f32)
            else:
                before = st[place - orows, :, n : n + CHUNK]
            state = before + sea[place, :, n : n + CHUNK] * full
            if step == OSTEPS - 1:
                for t in range(CHUNK // 128):
                    at = pl.ds(pl.multiple_of(local_row(place) * opad, 16), opad)
                    line[n // 128 + t, at, :] = state[
                        :, t * 128 : (t + 1) * 128]
            else:
                if orows <= place < 2 * orows:
                    st[place - orows, :, n : n + CHUNK] = state
                xs[center, n : n + CHUNK] = state.astype(bf16)

    last = 3 * orows - 3

    def first_one(k, carry):
        for i in range(2):
            spread_hidden(2 * k - 1 + i)
        for i in range(2):
            first(0, 1 + 2 * k + i)
        return carry

    def finished(place):
        at = pl.ds(pl.multiple_of(local_row(place) * opad, 16), opad)
        return pltpu.make_async_copy(
            line.at[:, at, :], line_hbm.at[:, at, :], out_sems.at[place - orows])

    lax.fori_loop(0, (last - 1) // 2, first_one, 0)
    for place in range(2, last - 1):
        if place < 4:
            spread_hidden(last - 4 + place)
        else:
            spread_state(place - 2, 0)
        second(0, place)
    for place in range(3, last - 2):
        if place < 5:
            spread_state(last - 6 + place, 0)
        else:
            spread_hidden(place - 2)
        first(1, place)

    for place in (last - 4, last - 3):
        spread_hidden(place)
    for place in range(orows, last - 3):
        second(1, place)
        finished(place).start()

    @pl.when(has_slow)
    def _():
        for place in range(2 * orows - 3, orows - 1, -1):
            halo_copy(SLOW, place).wait()

    for place in (last + 1, last + 2):
        spread_state(place, 0)
    for place in (last, last + 1):
        first(0, place, True)
    for place in (last, last + 1):
        spread_hidden(place)
    for place in (last - 1, last):
        second(0, place)
    for place in (last - 1, last):
        spread_state(place, 0)
    for place in (last - 2, last - 1):
        first(1, place)
    for place in (last - 2, last - 1):
        spread_hidden(place)
    for place in range(last - 3, last - 1):
        second(1, place)
        finished(place).start()
    for place in range(orows, last - 1):
        finished(place).wait()
    after_copy.wait()


def output_kernel(after_hbm, line_hbm, atmos_hbm, ocean_hbm, after, line, ocean, in_sems, out_sems):
    och, orows, olon = ocean.shape
    tiles = line.shape[0]
    opad = line.shape[1] // orows
    per_step = CHUNK // 128
    after_in = pltpu.make_async_copy(after_hbm, after, in_sems.at[tiles // per_step])
    after_out = pltpu.make_async_copy(after, atmos_hbm, out_sems.at[0])
    ocean_out = pltpu.make_async_copy(ocean, ocean_hbm, out_sems.at[1])
    ins = []
    for step in range(tiles // per_step):
        at = slice(step * per_step, (step + 1) * per_step)
        ins.append(pltpu.make_async_copy(line_hbm.at[at], line.at[at], in_sems.at[step]))
    for copy in ins:
        copy.start()
    after_in.start()
    for step in range(tiles // per_step):
        ins[step].wait()
        begin = step * CHUNK
        end = min(begin + CHUNK, olon)
        for c in range(och):
            cells = [
                line[step * per_step + t, pl.ds(c, orows, stride=opad), :] for t in range(per_step)]
            cells = jnp.concatenate(cells, axis=1)[:, 0 : end - begin]
            ocean[c, :, begin:end] = cells.astype(ocean.dtype)
    ocean_out.start()
    after_in.wait()
    after_out.start()
    ocean_out.wait()
    after_out.wait()


def local(
    atmos,
    ocean_state,
    land_mask,
    w_qkv,
    w_out,
    head_scale,
    gain_attn,
    gain_flux,
    w_flux,
    surf_embed,
    flux_start,
    flux_weight,
    surf_start,
    surf_weight,
    conv_first,
    conv_second,
):
    token_count, width = atmos.shape
    och, orows, olon = ocean_state.shape
    alon = olon // SPAN
    nflux = w_flux.shape[1]
    taps, hid, _ = conv_first.shape
    groups = width // GROUP
    per_group = GROUP // (width // head_scale.shape[0])
    padded = round_up(token_count, 16)
    key_pad = round_up(token_count, 128)
    opad = round_up(och, 16)
    wide = round_up(olon + 2, CHUNK)
    places = 3 * orows
    bf16 = jnp.bfloat16
    f32 = jnp.float32
    vmem = pl.BlockSpec(memory_space=pltpu.VMEM)
    smem = pl.BlockSpec(memory_space=pltpu.SMEM)
    anywhere = pl.BlockSpec(memory_space=pl.ANY)
    turned_shape = (round_up(taps * opad, 128), hid)
    after, line = pl.pallas_call(
        step_kernel,
        out_shape=[
            jax.ShapeDtypeStruct(atmos.shape, bf16),
            jax.ShapeDtypeStruct((wide // 128, orows * opad, 128), f32),
        ],
        in_specs=[smem] * 5 + [vmem] * 5 + [anywhere] * 6,
        out_specs=[anywhere] * 2,
        scratch_shapes=[
            pltpu.VMEM(ocean_state.shape, bf16),
            pltpu.VMEM(atmos.shape, bf16),
            pltpu.VMEM(atmos.shape, bf16),
            pltpu.VMEM((2, round_up(surf_weight.shape[1] + 1, 8), 128), f32),
            pltpu.VMEM((orows - 2, opad, wide), bf16),
            pltpu.VMEM((taps, och + nflux, hid), bf16),
            pltpu.VMEM(conv_second.shape, bf16),
            pltpu.VMEM((4, VARS * orows, alon), bf16),
            pltpu.VMEM((2, padded, width), bf16),
            pltpu.VMEM((groups, padded, GROUP), bf16),
            pltpu.VMEM((2, groups, padded, GROUP), bf16),
            pltpu.VMEM((2, groups, padded, GROUP), bf16),
            pltpu.VMEM((2, per_group * key_pad, 128), bf16),
            pltpu.VMEM((2, per_group * key_pad, GROUP), bf16),
            pltpu.VMEM((2, padded, per_group * key_pad), bf16),
            pltpu.VMEM((head_scale.shape[0], padded, 128), f32),
            pltpu.VMEM((width // 128, padded, GROUP), f32),
            pltpu.VMEM((alon, wide), bf16),
            pltpu.VMEM((3, nflux, alon), bf16),
            pltpu.VMEM((3, orows, nflux, alon), bf16),
            pltpu.VMEM((3, orows, olon), jnp.int32),
            pltpu.VMEM((places, 1, wide), f32),
            pltpu.VMEM(atmos.shape, bf16),
            pltpu.VMEM((wide // 128, orows * opad, 128), f32),
            pltpu.VMEM((places * 3 * opad, wide), bf16),
            pltpu.VMEM((places * 3 * nflux, wide), bf16),
            pltpu.VMEM((places * 3 * hid, wide), bf16),
            pltpu.VMEM((orows, opad, wide), f32),
            pltpu.VMEM(((places - 2) * hid, wide), f32),
            pltpu.VMEM(turned_shape, f32),
            pltpu.VMEM((hid, turned_shape[0]), bf16),
            pltpu.VMEM((hid, taps * nflux), bf16),
            pltpu.VMEM((opad, taps * hid), bf16),
            pltpu.SemaphoreType.DMA((7,)),
            pltpu.SemaphoreType.DMA((orows + 1,)),
            pltpu.SemaphoreType.DMA((7, 3)),
            pltpu.SemaphoreType.DMA((7, 3)),
            pltpu.SemaphoreType.DMA((2, groups)),
            pltpu.SemaphoreType.DMA((2, groups)),
            pltpu.SemaphoreType.DMA((3, orows)),
            pltpu.SemaphoreType.DMA((3, orows)),
        ],
        compiler_params=pltpu.CompilerParams(
            collective_id=0, has_side_effects=True, vmem_limit_bytes=63 * 1024 * 1024
        ),
        name="coupled_step",
    )(surf_start, surf_weight, flux_start, flux_weight.T, head_scale, land_mask, surf_embed,
      gain_attn[None, :], gain_flux[None, :], w_flux.T, atmos, ocean_state, w_qkv, w_out,
      conv_first.transpose(0, 2, 1), conv_second)
    return pl.pallas_call(
        output_kernel,
        out_shape=[
            jax.ShapeDtypeStruct(atmos.shape, bf16),
            jax.ShapeDtypeStruct(ocean_state.shape, bf16),
        ],
        in_specs=[anywhere] * 2,
        out_specs=[anywhere] * 2,
        scratch_shapes=[
            pltpu.VMEM(atmos.shape, bf16),
            pltpu.VMEM(line.shape, f32),
            pltpu.VMEM(ocean_state.shape, bf16),
            pltpu.SemaphoreType.DMA((wide // CHUNK + 1,)),
            pltpu.SemaphoreType.DMA((2,)),
        ],
        name="outputs",
    )(after, line)


def solution(mesh):
    in_specs = (
        P(("ens", "lat"), None),
        P(None, ("ens", "lat"), None),
        P("lat", None),
        P(),
        P(),
        P(),
        P(),
        P(),
        P(),
        P(),
        P("lat"),
        P("lat", None),
        P("lat"),
        P("lat", None),
        P(),
        P(),
    )
    out_specs = (P(("ens", "lat"), None), P(None, ("ens", "lat"), None))
    return jax.shard_map(local, mesh=mesh, in_specs=in_specs, out_specs=out_specs, check_vma=False)
```

```python
import jax
import jax.numpy as jnp
from jax import lax
from jax.experimental import pallas as pl
from jax.experimental.pallas import tpu as pltpu
from jax.sharding import PartitionSpec as P

LEVELS = 19
VARS = 4
SPAN = 4
OSTEPS = 2
GROUP = 256
CHUNK = 512
FAST, OWN, SLOW = 0, 1, 2


def round_up(value, unit):
    return (value + unit - 1) // unit * unit


def rms_norm(values, scaling):
    return values * lax.rsqrt(jnp.mean(values * values, axis=-1, keepdims=True) + 1e-06) * scaling


def step_kernel(surf_first, surf_weight, flux_first, flux_weight, scale_ref, land_ref, embed_ref,
                gain_ref, flux_gain_ref, wflux_ref, atmos_hbm, ocean_hbm, qkv_hbm, wout_hbm,
                first_hbm, second_hbm,
                after_hbm, line_hbm,
                ocean_in, atmos_in, atmos_near, factors, edge, first_in, second_in, surf, near, queries, keys, vals, keys_wide,
                vals_wide, probs, largest_at, gathered, repeat, rows, mid, land, sea,
                after_out, line, xs, fx, hs, st, kept, turned, w_state, w_flux, w_second,
                load_sems, out_sems, send_sems, recv_sems, kv_send, kv_recv, halo_send, halo_recv):
    me = lax.axis_index("lat")
    count = lax.axis_size("lat")
    odd = me % 2
    even = 1 - odd
    fast = me + 1 - 2 * odd
    slow = me - 1 + 2 * odd
    has_slow = (slow >= 0) & (slow < count)
    target = {FAST: fast, SLOW: slow}
    token_count, width = atmos_in.shape
    groups = width // GROUP
    depth = width // scale_ref.shape[0]
    per_group = GROUP // depth
    padded = near.shape[1]
    per_tile = 128 // depth
    key_pad = keys_wide.shape[1] // per_group
    och, orows, olon = ocean_in.shape
    wide = xs.shape[1]
    tiles = wide // 128
    nflux = wflux_ref.shape[0]
    taps, _, hid = first_in.shape
    opad = w_second.shape[0]
    alon = olon // SPAN
    tail = wide - 128
    first_pad = olon - tail
    total_rows = count * orows
    band = surf_weight.shape[1]
    beyond_slow = slow - 1 + 2 * odd
    bf16 = jnp.bfloat16
    f32 = jnp.float32

    def send(kind, side, source, dest):
        return pltpu.make_async_remote_copy(
            src_ref=source, dst_ref=dest, send_sem=send_sems.at[kind, side],
            recv_sem=recv_sems.at[kind, side], device_id={"lat": target[side]},
            device_id_type=pl.DeviceIdType.MESH,
        )

    def start_both(kind, source, dest):
        send(kind, FAST, source, dest(FAST)).start()

        @pl.when(has_slow)
        def _():
            send(kind, SLOW, source, dest(SLOW)).start()

    def wait_both(kind, source, dest):
        send(kind, FAST, source, dest(FAST)).wait()

        @pl.when(has_slow)
        def _():
            send(kind, SLOW, source, dest(SLOW)).wait()

    def local_row(place):
        return odd * (place - orows) + even * (2 * orows - 1 - place)

    half_width = qkv_hbm.shape[1] // 2
    loads = (
        pltpu.make_async_copy(ocean_hbm, ocean_in, load_sems.at[0]),
        pltpu.make_async_copy(atmos_hbm, atmos_in, load_sems.at[1]),
        pltpu.make_async_copy(qkv_hbm.at[:, 0:half_width], hs.at[0:width, :], load_sems.at[2]),
        pltpu.make_async_copy(
            qkv_hbm.at[:, half_width:], hs.at[width : 2 * width, :], load_sems.at[3]),
        pltpu.make_async_copy(wout_hbm, hs.at[2 * width : 3 * width, 0:width], load_sems.at[4]),
        pltpu.make_async_copy(first_hbm, first_in, load_sems.at[5]),
        pltpu.make_async_copy(second_hbm, second_in, load_sems.at[6]),
    )
    for load in loads:
        load.start()
    barrier = pltpu.get_barrier_semaphore()
    pl.semaphore_signal(
        barrier, inc=1, device_id={"lat": fast}, device_id_type=pl.DeviceIdType.MESH)

    @pl.when(has_slow)
    def _():
        pl.semaphore_signal(
            barrier, inc=1, device_id={"lat": slow}, device_id_type=pl.DeviceIdType.MESH)

    @pl.when(jnp.logical_not(has_slow))
    def _():
        surf[SLOW] = jnp.zeros_like(surf[SLOW])
        rows[SLOW] = jnp.zeros_like(rows[SLOW])
        mid[SLOW] = jnp.zeros_like(mid[SLOW])
        land[SLOW] = jnp.zeros_like(land[SLOW])
        for i in range(orows):
            base = (2 * orows + i) * 3 * opad + opad
            xs[base : base + opad, :] = jnp.zeros((opad, wide), bf16)

    column = lax.broadcasted_iota(jnp.int32, (alon, wide), 1)
    longitude = jnp.where(column < olon, column, jnp.where(column == olon, 0, olon - 1))
    first_column = lax.broadcasted_iota(jnp.int32, (alon, wide), 0) * SPAN
    chosen = (longitude >= first_column) & (longitude < first_column + SPAN)
    repeat[...] = jnp.where(chosen, 1.0, 0.0).astype(bf16)
    row_at = lax.broadcasted_iota(jnp.int32, factors.shape[1:], 0)
    filled = jnp.where(row_at == band, surf_first[0].astype(f32), 0.0)
    for b in range(band):
        filled = jnp.where(row_at == b, surf_weight[0, b], filled)
    factors[0] = filled
    loads[0].wait()
    top = jnp.concatenate(
        [ocean_in[v * LEVELS].astype(f32) for v in range(VARS)], axis=0).astype(bf16)
    summed = lax.dot_general(
        top, repeat[:, 0:olon], (((1,), (1,)), ((), ())), preferred_element_type=f32)
    surf[OWN] = (summed * (1.0 / SPAN)).astype(bf16)
    land[OWN] = land_ref[...]
    pl.semaphore_wait(barrier, 1 + jnp.where(has_slow, 1, 0))

    def surf_at(side):
        return surf.at[side]

    def land_at(side):
        return land.at[side]

    start_both(0, surf.at[OWN], surf_at)

    @pl.when(has_slow)
    def _():
        send(6, SLOW, factors.at[0], factors.at[1]).start()

    start_both(1, land_ref, land_at)

    for c in range(opad):
        if c < och:
            cells = jnp.concatenate(
                [ocean_in[c].astype(f32), jnp.zeros((orows, wide - olon), f32)], axis=1)
        else:
            cells = jnp.zeros((orows, wide), f32)
        for t in range(tiles):
            line[t, pl.ds(c, orows, stride=opad), :] = cells[
                :, t * 128 : (t + 1) * 128]
    for place in range(orows, 2 * orows):
        base = place * 3 * opad + opad
        for t in range(tiles):
            at = pl.multiple_of(local_row(place) * opad, 16)
            xs[base : base + opad, t * 128 : (t + 1) * 128] = line[t, pl.ds(at, opad), :].astype(bf16)
        if place < 2 * orows - 2:
            edge[place - orows] = xs[base : base + opad, :]

    def spread(ref, base, size):
        center = pl.ds(base + size, size)
        head = ref[center, 0:128]
        last = ref[center, tail:]
        at = lax.broadcasted_iota(jnp.int32, last.shape, 1)
        end = pltpu.roll(last, 128 - first_pad, 1)
        begin = pltpu.roll(head, first_pad, 1)
        last = jnp.where(at == first_pad, begin, jnp.where(at == 127, end, last))
        whole = jnp.concatenate([ref[center, 0:tail], last], axis=1)
        ref[pl.ds(base, size), :] = pltpu.roll(whole, 1, 1)
        ref[pl.ds(base + 2 * size, size), :] = pltpu.roll(whole, wide - 1, 1)

    def spread_state(place, carry):
        spread(xs, pl.multiple_of(place * 3 * opad, 16), opad)
        return carry

    def spread_hidden(place):
        spread(hs, pl.multiple_of((place + 1) * 3 * hid, 16), hid)

    lane = lax.broadcasted_iota(jnp.int32, (1, GROUP), 1) // depth
    half_lane = lax.broadcasted_iota(jnp.int32, (1, 128), 1) // depth
    stat_lane = lax.broadcasted_iota(jnp.int32, (1, 128), 1)

    keys_wide[...] = jnp.zeros_like(keys_wide)
    vals_wide[...] = jnp.zeros_like(vals_wide)
    for h in range(per_group):
        counted = jnp.where(half_lane == h % per_tile, 1.0, 0.0).astype(bf16)
        for slot in range(2):
            vals_wide[slot, h * key_pad : h * key_pad + padded, 128:] = jnp.broadcast_to(
                counted, (padded, 128))

    lax.fori_loop(orows, 2 * orows, spread_state, 0)

    loads[5].wait()
    loads[6].wait()
    turned[...] = jnp.zeros_like(turned)
    row_id = lax.broadcasted_iota(jnp.int32, (opad, hid), 0)
    for k in range(taps):
        source = (odd * (k // 3) + even * (2 - k // 3)) * 3 + k % 3
        tap = first_in[source].astype(f32)
        turned[k * opad : (k + 1) * opad, :] = jnp.where(row_id < och, tap[0:opad], 0.0)
    w_state[...] = turned[...].T.astype(bf16)
    turned[...] = jnp.zeros_like(turned)
    for k in range(taps):
        source = (odd * (k // 3) + even * (2 - k // 3)) * 3 + k % 3
        turned[k * nflux : (k + 1) * nflux, :] = first_in[source].astype(f32)[och:]
        w_second[0:och, k * hid : (k + 1) * hid] = second_in[source]
        w_second[och:, k * hid : (k + 1) * hid] = jnp.zeros((opad - och, hid), bf16)
    w_flux[...] = turned[0 : w_flux.shape[1], :].T.astype(bf16)

    embed = jnp.concatenate(
        [jnp.broadcast_to(embed_ref[v : v + 1, :], (orows, width)) for v in range(VARS)], axis=0)
    which = lax.broadcasted_iota(jnp.int32, (VARS * orows, 128), 0) % orows

    def start_of(tokens, whose, parts, devices):
        starts = factors[whose, band : band + 1, :]
        scaled = []
        for device in devices:
            column = which + device * orows
            weights = jnp.zeros((VARS * orows, 128), f32)
            for b in range(band):
                weights = weights + jnp.where(
                    column.astype(f32) == starts + b, factors[whose, b : b + 1, :], 0.0)
            weights = jnp.where((column >= 0) & (column < total_rows), weights, 0.0)
            scaled.append(jnp.concatenate([weights] * (width // 128), axis=1) * embed)
        scaled = jnp.concatenate(scaled, axis=0)
        high = scaled.astype(bf16)
        rest = scaled - high.astype(f32)
        middle = rest.astype(bf16)
        low = (rest - middle.astype(f32)).astype(bf16)
        fields = jnp.concatenate([surf[part] for part in parts] * 3, axis=0)
        started = tokens[...].astype(f32) + lax.dot_general(
            fields, jnp.concatenate([high, middle, low], axis=0),
            (((0,), (0,)), ((), ())), preferred_element_type=f32)
        return jnp.concatenate([started, jnp.zeros((padded - token_count, width), f32)], axis=0)

    loads[1].wait()
    wait_both(0, surf.at[OWN], surf_at)

    @pl.when(has_slow)
    def _():
        send(2, SLOW, atmos_hbm, atmos_near).start()

    started = start_of(atmos_in, 0, (FAST, OWN, SLOW), (fast, me, slow))
    held = kept.at[0:padded, 0:width]
    held[...] = started
    near[0] = rms_norm(started, gain_ref[...]).astype(bf16)

    def halo_copy(side, place):
        goal = {FAST: 2 * orows - 1, SLOW: 4 * orows - 1}[side] - place
        source = xs.at[pl.ds(place * 3 * opad + opad, opad), :]
        if side == SLOW and place < 2 * orows - 2:
            source = edge.at[place - orows]
        dest = xs.at[pl.ds(goal * 3 * opad + opad, opad), :]
        return pltpu.make_async_remote_copy(
            src_ref=source, dst_ref=dest, send_sem=halo_send.at[side, place - orows],
            recv_sem=halo_recv.at[side, place - orows], device_id={"lat": target[side]},
            device_id_type=pl.DeviceIdType.MESH,
        )

    @pl.when(has_slow)
    def _():
        send(5, SLOW, surf.at[FAST], surf.at[3]).start()
        for place in (2 * orows - 1, 2 * orows - 2):
            halo_copy(SLOW, place).start()

    blocks = (slice(0, padded),)
    ones_at = lax.broadcasted_iota(jnp.int32, (GROUP, 128), 0) % 128 // depth
    ones = jnp.where(ones_at == half_lane, 1.0, 0.0).astype(bf16)

    def head_scales(raw):
        pieces = []
        for t in range(GROUP // 128):
            piece = raw[:, t * 128 : (t + 1) * 128]
            squares = piece * piece
            coarse = squares.astype(bf16)
            fine = (squares - coarse.astype(f32)).astype(bf16)
            total = jnp.dot(
                jnp.concatenate([coarse, fine], axis=1), ones, preferred_element_type=f32)
            pieces.append(piece * lax.rsqrt(total * (1.0 / depth) + 1e-06))
        return jnp.concatenate(pieces, axis=1)

    def project(part, column, block):
        at = pl.ds(pl.multiple_of((column // half_width) * width, width), width)
        columns = pl.ds(pl.multiple_of(column % half_width, GROUP), GROUP)
        return jnp.dot(near[part, block, :], hs[at, columns], preferred_element_type=f32)

    beyond = stat_lane + (key_pad - 128) >= token_count

    def attend(g, key, value, fresh, slot):
        for h in range(per_group):
            columns = slice(h // per_tile * 128, (h // per_tile + 1) * 128)
            at = slice(h * key_pad, h * key_pad + padded)
            mine = half_lane == h % per_tile
            keys_wide[slot, at, :] = jnp.where(mine, key[:, columns], jnp.zeros((1, 128), bf16))
            vals_wide[slot, at, 0:128] = jnp.where(
                mine, value[:, columns], jnp.zeros((1, 128), bf16))
        for t in range(per_group // per_tile):
            both = slice(t * per_tile * key_pad, (t + 1) * per_tile * key_pad)
            where = g * (per_group // per_tile) + t
            for block in blocks:
                size = block.stop - block.start
                scores = lax.dot_general(
                    queries[g, block, t * 128 : (t + 1) * 128], keys_wide[slot, both, :],
                    (((1,), (1,)), ((), ())), preferred_element_type=f32)
                fade = None
                raised = []
                for j in range(per_tile):
                    at = g * per_group + t * per_tile + j
                    base = j * key_pad
                    pieces = [scores[:, base + i : base + i + 128] for i in range(0, key_pad, 128)]
                    pieces[-1] = jnp.where(beyond, -1e30, pieces[-1])
                    largest = pieces[0]
                    for piece in pieces[1:]:
                        largest = jnp.maximum(largest, piece)
                    largest = jnp.broadcast_to(jnp.max(largest, axis=1, keepdims=True), (size, 128))
                    if not fresh:
                        before = largest_at[at, block, :]
                        largest = jnp.maximum(largest, before)
                        factor = jnp.exp(before - largest)
                        fade = factor if fade is None else jnp.where(half_lane == j, factor, fade)
                    largest_at[at, block, :] = largest
                    raised += [jnp.exp(piece - largest) for piece in pieces]
                probs[slot, block, both] = jnp.concatenate(raised, axis=1).astype(bf16)
                mixed = jnp.dot(
                    probs[slot, block, both], vals_wide[slot, both, :], preferred_element_type=f32)
                if fresh:
                    gathered[where, block, :] = mixed
                else:
                    gathered[where, block, 0:128] = (
                        gathered[where, block, 0:128] * fade + mixed[:, 0:128])
                    gathered[where, block, 128:] = (
                        gathered[where, block, 128:] * fade + mixed[:, 128:])

    def kv_copy(g, kind):
        ref = (keys, vals)[kind]
        return pltpu.make_async_remote_copy(
            src_ref=ref.at[0, g], dst_ref=ref.at[1, g], send_sem=kv_send.at[kind, g],
            recv_sem=kv_recv.at[kind, g], device_id={"lat": fast},
            device_id_type=pl.DeviceIdType.MESH,
        )

    def by_two(body):
        def run(i, carry):
            for slot in range(2):
                body(2 * i + slot, slot)
            return carry
        lax.fori_loop(0, groups // 2, run, 0)

    def own(g, slot):
        column = g * GROUP
        scale = jnp.zeros((1, GROUP), f32)
        for h in range(per_group):
            scale = jnp.where(lane == h, scale_ref[g * per_group + h], scale)
        for block in blocks:
            query = head_scales(project(0, column, block))
            queries[g, block, :] = (query * (scale * (1.0 / depth**0.5))).astype(bf16)
            keys[0, g, block, :] = head_scales(project(0, width + column, block)).astype(bf16)
            vals[0, g, block, :] = project(0, 2 * width + column, block).astype(bf16)
        for kind in range(2):
            kv_copy(g, kind).start()
        attend(g, keys[0, g], vals[0, g], True, slot)

    loads[2].wait()
    loads[3].wait()
    by_two(own)
    for place in range(orows, 2 * orows):
        halo_copy(FAST, place).start()

    def from_fast(g, slot):
        for kind in range(2):
            kv_copy(g, kind).wait()
        attend(g, keys[1, g], vals[1, g], False, slot)

    by_two(from_fast)

    @pl.when(has_slow)
    def _():
        send(2, SLOW, atmos_hbm, atmos_near).wait()
        send(5, SLOW, surf.at[FAST], surf.at[3]).wait()
        send(6, SLOW, factors.at[0], factors.at[1]).wait()
        near[1] = rms_norm(start_of(
            atmos_near, 1, (3, SLOW, OWN), (beyond_slow, slow, me)), gain_ref[...]).astype(bf16)

    def from_slow(g, slot):
        column = g * GROUP
        key = jnp.concatenate(
            [head_scales(project(1, width + column, block)) for block in blocks], axis=0).astype(bf16)
        value = jnp.concatenate(
            [project(1, 2 * width + column, block) for block in blocks], axis=0).astype(bf16)
        attend(g, key, value, False, slot)

    @pl.when(has_slow)
    def _():
        by_two(from_slow)

    for place in range(orows, 2 * orows):
        halo_copy(FAST, place).wait()
    loads[4].wait()
    for place in range(orows):
        spread_state(place, 0)

    for t in range(width // 128):
        near[0, :, t * 128 : (t + 1) * 128] = (
            gathered[t, :, 0:128] * (1.0 / gathered[t, :, 128:])).astype(bf16)
    pieces = []
    for n in range(0, width, CHUNK):
        piece = held[:, n : n + CHUNK] + jnp.dot(
            near[0], hs[2 * width : 3 * width, n : n + CHUNK], preferred_element_type=f32)
        pieces.append(piece[0:token_count])
    after = jnp.concatenate(pieces, axis=1)
    after_out[...] = after.astype(bf16)
    after_copy = pltpu.make_async_copy(after_out, after_hbm, out_sems.at[orows])
    after_copy.start()
    flux_in = rms_norm(after, flux_gain_ref[...]).astype(bf16)
    rows[OWN] = lax.dot_general(
        wflux_ref[...], flux_in, (((1,), (1,)), ((), ())), preferred_element_type=f32
    ).astype(bf16)

    def rows_at(side):
        return rows.at[side]

    start_both(3, rows.at[OWN], rows_at)


    wait_both(1, land_ref, land_at)
    for side, base in ((FAST, 0), (OWN, orows), (SLOW, 2 * orows)):
        for i in range(orows):
            place = base + i
            if side == OWN:
                at = local_row(place)
            else:
                at = odd * i + even * (orows - 1 - i)
            cells = land[side, pl.ds(at, 1), :].astype(f32)
            sea[place, :, 0:tail] = cells[:, 0:tail]
            sea[place, :, tail:] = jnp.concatenate(
                [cells[:, tail:], jnp.zeros((1, wide - olon), f32)], axis=1)
    @pl.when(has_slow)
    def _():
        for place in (2 * orows - 1, 2 * orows - 2):
            halo_copy(SLOW, place).wait()

    def state_part(place, n):
        block = xs[pl.ds(pl.multiple_of((place - 1) * 3 * opad, 16), 9 * opad), n : n + CHUNK]
        return jnp.dot(w_state[:, 0 : 9 * opad], block, preferred_element_type=f32)

    def keep_state(place, carry):
        for n in range(0, wide, CHUNK):
            kept[pl.ds(pl.multiple_of((place - 1) * hid, 16), hid), n : n + CHUNK] = state_part(
                place, n)
        return carry

    def keep_first(i, carry):
        spread_state(2 * orows + i, 0)
        for j in range(2):
            keep_state(1 + 2 * i + j, 0)
        return carry

    lax.fori_loop(0, 2, keep_first, 0)
    wait_both(3, rows.at[OWN], rows_at)
    sources = [rows[side].astype(f32) for side in range(3)]
    for i in range(orows):
        at = local_row(orows + i)
        regridded = jnp.zeros_like(sources[0])
        for side, device in ((FAST, fast), (OWN, me), (SLOW, slow)):
            weight = jnp.float32(0.0)
            for b in range(flux_weight.shape[0]):
                weight = weight + jnp.where(
                    flux_first[at] + b == device, flux_weight[b, at], 0.0)
            regridded = regridded + weight * sources[side]
        mid[OWN, i] = regridded.astype(bf16)

    def mid_at(side):
        return mid.at[side]

    start_both(4, mid.at[OWN], mid_at)

    lax.fori_loop(orows + 1, 2 * orows + 1, keep_state, 0, unroll=2)
    wait_both(4, mid.at[OWN], mid_at)

    @pl.when(has_slow)
    def _():
        for place in range(2 * orows - 3, orows - 1, -1):
            halo_copy(SLOW, place).start()

    every = [mid[FAST, orows - 1 - i] for i in range(orows)]
    every += [mid[OWN, i] for i in range(orows)]
    every += [mid[SLOW, orows - 1 - i] for i in range(orows)]
    repeated = jnp.dot(
        jnp.concatenate(every, axis=0), repeat[...], preferred_element_type=f32).astype(bf16)
    for place in range(3 * orows):
        base = place * 3 * nflux
        whole = repeated[place * nflux : (place + 1) * nflux]
        fx[base + nflux : base + 2 * nflux, :] = whole
        fx[base : base + nflux, :] = pltpu.roll(whole, 1, 1)
        fx[base + 2 * nflux : base + 3 * nflux, :] = pltpu.roll(whole, wide - 1, 1)

    root = (2.0 / jnp.pi) ** 0.5

    def inside_of(place):
        row = me * orows + local_row(place)
        return (row >= 0) & (row < total_rows)

    def first(step, place, both=False):
        half = jnp.where(inside_of(place), 0.5, 0.0).astype(f32)
        at = pl.ds(pl.multiple_of((place - 1) * hid, 16), hid)
        for n in range(0, wide, CHUNK):
            if step == 0:
                block = fx[
                    pl.ds(pl.multiple_of((place - 1) * 3 * nflux, 16), 9 * nflux), n : n + CHUNK]
                share = jnp.dot(w_flux[...], block, preferred_element_type=f32)
                full = share + (state_part(place, n) if both else kept[at, n : n + CHUNK])
                kept[at, n : n + CHUNK] = share
            else:
                full = kept[at, n : n + CHUNK] + state_part(place, n)
            bent = jnp.tanh(full * (root + (root * 0.044715) * (full * full)))
            half_full = full * half
            hidden = half_full + half_full * bent
            hs[pl.ds(pl.multiple_of((place + 1) * 3 * hid + hid, 16), hid), n : n + CHUNK] = (
                hidden.astype(bf16))

    def second(step, place):
        for n in range(0, wide, CHUNK):
            block = hs[pl.ds(pl.multiple_of(place * 3 * hid, 16), 9 * hid), n : n + CHUNK]
            full = jnp.dot(w_second[...], block, preferred_element_type=f32)
            center = pl.ds(pl.multiple_of(place * 3 * opad + opad, 16), opad)
            if step == 0:
                before = xs[center, n : n + CHUNK].astype(f32)
            else:
                before = st[place - orows, :, n : n + CHUNK]
            state = before + sea[place, :, n : n + CHUNK] * full
            if step == OSTEPS - 1:
                for t in range(CHUNK // 128):
                    at = pl.ds(pl.multiple_of(local_row(place) * opad, 16), opad)
                    line[n // 128 + t, at, :] = state[
                        :, t * 128 : (t + 1) * 128]
            else:
                if orows <= place < 2 * orows:
                    st[place - orows, :, n : n + CHUNK] = state
                xs[center, n : n + CHUNK] = state.astype(bf16)

    last = 3 * orows - 3

    def first_one(k, carry):
        for i in range(2):
            spread_hidden(2 * k - 1 + i)
        for i in range(2):
            first(0, 1 + 2 * k + i)
        return carry

    def finished(place):
        at = pl.ds(pl.multiple_of(local_row(place) * opad, 16), opad)
        return pltpu.make_async_copy(
            line.at[:, at, :], line_hbm.at[:, at, :], out_sems.at[place - orows])

    lax.fori_loop(0, (last - 1) // 2, first_one, 0)
    for place in range(2, last - 1):
        if place < 4:
            spread_hidden(last - 4 + place)
        else:
            spread_state(place - 2, 0)
        second(0, place)
    for place in range(3, last - 2):
        if place < 5:
            spread_state(last - 6 + place, 0)
        else:
            spread_hidden(place - 2)
        first(1, place)

    for place in (last - 4, last - 3):
        spread_hidden(place)
    for place in range(orows, last - 3):
        second(1, place)
        finished(place).start()

    @pl.when(has_slow)
    def _():
        for place in range(2 * orows - 3, orows - 1, -1):
            halo_copy(SLOW, place).wait()

    for place in (last + 1, last + 2):
        spread_state(place, 0)
    for place in (last, last + 1):
        first(0, place, True)
    for place in (last, last + 1):
        spread_hidden(place)
    for place in (last - 1, last):
        second(0, place)
    for place in (last - 1, last):
        spread_state(place, 0)
    for place in (last - 2, last - 1):
        first(1, place)
    for place in (last - 2, last - 1):
        spread_hidden(place)
    for place in range(last - 3, last - 1):
        second(1, place)
        finished(place).start()
    for place in range(orows, last - 1):
        finished(place).wait()
    after_copy.wait()


def output_kernel(after_hbm, line_hbm, atmos_hbm, ocean_hbm, after, line, ocean, in_sems, out_sems):
    och, orows, olon = ocean.shape
    tiles = line.shape[0]
    opad = line.shape[1] // orows
    per_step = CHUNK // 128
    after_in = pltpu.make_async_copy(after_hbm, after, in_sems.at[tiles // per_step])
    after_out = pltpu.make_async_copy(after, atmos_hbm, out_sems.at[0])
    ocean_out = pltpu.make_async_copy(ocean, ocean_hbm, out_sems.at[1])
    ins = []
    for step in range(tiles // per_step):
        at = slice(step * per_step, (step + 1) * per_step)
        ins.append(pltpu.make_async_copy(line_hbm.at[at], line.at[at], in_sems.at[step]))
    for copy in ins:
        copy.start()
    after_in.start()
    for step in range(tiles // per_step):
        ins[step].wait()
        begin = step * CHUNK
        end = min(begin + CHUNK, olon)
        for c in range(och):
            cells = [
                line[step * per_step + t, pl.ds(c, orows, stride=opad), :] for t in range(per_step)]
            cells = jnp.concatenate(cells, axis=1)[:, 0 : end - begin]
            ocean[c, :, begin:end] = cells.astype(ocean.dtype)
    ocean_out.start()
    after_in.wait()
    after_out.start()
    ocean_out.wait()
    after_out.wait()


def local(
    atmos,
    ocean_state,
    land_mask,
    w_qkv,
    w_out,
    head_scale,
    gain_attn,
    gain_flux,
    w_flux,
    surf_embed,
    flux_start,
    flux_weight,
    surf_start,
    surf_weight,
    conv_first,
    conv_second,
):
    token_count, width = atmos.shape
    och, orows, olon = ocean_state.shape
    alon = olon // SPAN
    nflux = w_flux.shape[1]
    taps, hid, _ = conv_first.shape
    groups = width // GROUP
    per_group = GROUP // (width // head_scale.shape[0])
    padded = round_up(token_count, 16)
    key_pad = round_up(token_count, 128)
    opad = round_up(och, 16)
    wide = round_up(olon + 2, CHUNK)
    places = 3 * orows
    bf16 = jnp.bfloat16
    f32 = jnp.float32
    vmem = pl.BlockSpec(memory_space=pltpu.VMEM)
    smem = pl.BlockSpec(memory_space=pltpu.SMEM)
    anywhere = pl.BlockSpec(memory_space=pl.ANY)
    turned_shape = (round_up(taps * opad, 128), hid)
    after, line = pl.pallas_call(
        step_kernel,
        out_shape=[
            jax.ShapeDtypeStruct(atmos.shape, bf16),
            jax.ShapeDtypeStruct((wide // 128, orows * opad, 128), f32),
        ],
        in_specs=[smem] * 5 + [vmem] * 5 + [anywhere] * 6,
        out_specs=[anywhere] * 2,
        scratch_shapes=[
            pltpu.VMEM(ocean_state.shape, bf16),
            pltpu.VMEM(atmos.shape, bf16),
            pltpu.VMEM(atmos.shape, bf16),
            pltpu.VMEM((2, round_up(surf_weight.shape[1] + 1, 8), 128), f32),
            pltpu.VMEM((orows - 2, opad, wide), bf16),
            pltpu.VMEM((taps, och + nflux, hid), bf16),
            pltpu.VMEM(conv_second.shape, bf16),
            pltpu.VMEM((4, VARS * orows, alon), bf16),
            pltpu.VMEM((2, padded, width), bf16),
            pltpu.VMEM((groups, padded, GROUP), bf16),
            pltpu.VMEM((2, groups, padded, GROUP), bf16),
            pltpu.VMEM((2, groups, padded, GROUP), bf16),
            pltpu.VMEM((2, per_group * key_pad, 128), bf16),
            pltpu.VMEM((2, per_group * key_pad, GROUP), bf16),
            pltpu.VMEM((2, padded, per_group * key_pad), bf16),
            pltpu.VMEM((head_scale.shape[0], padded, 128), f32),
            pltpu.VMEM((width // 128, padded, GROUP), f32),
            pltpu.VMEM((alon, wide), bf16),
            pltpu.VMEM((3, nflux, alon), bf16),
            pltpu.VMEM((3, orows, nflux, alon), bf16),
            pltpu.VMEM((3, orows, olon), jnp.int32),
            pltpu.VMEM((places, 1, wide), f32),
            pltpu.VMEM(atmos.shape, bf16),
            pltpu.VMEM((wide // 128, orows * opad, 128), f32),
            pltpu.VMEM((places * 3 * opad, wide), bf16),
            pltpu.VMEM((places * 3 * nflux, wide), bf16),
            pltpu.VMEM((places * 3 * hid, wide), bf16),
            pltpu.VMEM((orows, opad, wide), f32),
            pltpu.VMEM(((places - 2) * hid, wide), f32),
            pltpu.VMEM(turned_shape, f32),
            pltpu.VMEM((hid, turned_shape[0]), bf16),
            pltpu.VMEM((hid, taps * nflux), bf16),
            pltpu.VMEM((opad, taps * hid), bf16),
            pltpu.SemaphoreType.DMA((7,)),
            pltpu.SemaphoreType.DMA((orows + 1,)),
            pltpu.SemaphoreType.DMA((7, 3)),
            pltpu.SemaphoreType.DMA((7, 3)),
            pltpu.SemaphoreType.DMA((2, groups)),
            pltpu.SemaphoreType.DMA((2, groups)),
            pltpu.SemaphoreType.DMA((3, orows)),
            pltpu.SemaphoreType.DMA((3, orows)),
        ],
        compiler_params=pltpu.CompilerParams(
            collective_id=0, has_side_effects=True, vmem_limit_bytes=63 * 1024 * 1024
        ),
        name="coupled_step",
    )(surf_start, surf_weight, flux_start, flux_weight.T, head_scale, land_mask, surf_embed,
      gain_attn[None, :], gain_flux[None, :], w_flux.T, atmos, ocean_state, w_qkv, w_out,
      conv_first.transpose(0, 2, 1), conv_second)
    return pl.pallas_call(
        output_kernel,
        out_shape=[
            jax.ShapeDtypeStruct(atmos.shape, bf16),
            jax.ShapeDtypeStruct(ocean_state.shape, bf16),
        ],
        in_specs=[anywhere] * 2,
        out_specs=[anywhere] * 2,
        scratch_shapes=[
            pltpu.VMEM(atmos.shape, bf16),
            pltpu.VMEM(line.shape, f32),
            pltpu.VMEM(ocean_state.shape, bf16),
            pltpu.SemaphoreType.DMA((wide // CHUNK + 1,)),
            pltpu.SemaphoreType.DMA((2,)),
        ],
        name="outputs",
    )(after, line)


def solution(mesh):
    in_specs = (
        P(("ens", "lat"), None),
        P(None, ("ens", "lat"), None),
        P("lat", None),
        P(),
        P(),
        P(),
        P(),
        P(),
        P(),
        P(),
        P("lat"),
        P("lat", None),
        P("lat"),
        P("lat", None),
        P(),
        P(),
    )
    out_specs = (P(("ens", "lat"), None), P(None, ("ens", "lat"), None))
    return jax.shard_map(local, mesh=mesh, in_specs=in_specs, out_specs=out_specs, check_vma=False)
```
